256 devices in a mesh: seq: 32 (over x, z), head: 8 (over y, core).
Axes of the slice: x: 4, y: 4, z: 8, core: 2. Of those that a mesh axis runs over, the one named last changes fastest.
Arguments:
- queries: bfloat16 [2, 8192, 2048], P(None, 'seq', 'head'), may hold values from -1.75 to 1.75
- keys: bfloat16 [2, 8192, 2048], P(None, 'seq', 'head'), may hold values from -1.75 to 1.75
- values: bfloat16 [2, 8192, 2048], P(None, 'seq', 'head'), may hold values from -6 to 6
- gate_pre: bfloat16 [2, 8192, 2048], P(None, 'seq', 'head'), may hold values from -8 to 8
- grad_out: bfloat16 [2, 8192, 4096], P(None, 'seq', 'head'), may hold values from -6 to 6
- w_query: bfloat16 [4096, 2048], P(None, 'head'), may hold values from -0.09375 to 0.09375
- w_key: bfloat16 [4096, 2048], P(None, 'head'), may hold values from -0.09375 to 0.09375
- w_value: bfloat16 [4096, 2048], P(None, 'head'), may hold values from -0.09375 to 0.09375
- w_gate: bfloat16 [4096, 2048], P(None, 'head'), may hold values from -0.09375 to 0.09375
- w_out: bfloat16 [2048, 4096], P('head'), may hold values from -0.125 to 0.125
Outputs:
- grad_in: bfloat16 [2, 8192, 4096], P(None, 'seq', 'head')
The draws below stay inside these ranges and needn't reach their ends.
All inputs are finite; a program needn't handle non-finite values.
Results may differ from the reference program's by a relative error of at most 0.022.
Values may be sent and summed in bfloat16 or wider, within the bound.
No kernel may reach another device: no remote copies, remote signals or barrier semaphores. Data moves between devices by JAX's collectives and lax.ppermute only.
A program may use at most 128 MiB of HBM per device.

```python
import jax
import jax.numpy as jnp
from jax import lax

D = 4096
HD = 128
HEADS = 16
SPAN = 256
SEQS = 2
LENGTH = 8192
N_HEAD = 8


def levels(stream_key, shape, split, least, high):
    factor_of, own = 1.0, jax.random.fold_in(stream_key, 6)
    for axis_at, shards_of in split:
        draws = jnp.exp(jax.random.uniform(jax.random.fold_in(own, axis_at), (shards_of,), jnp.float32, least / len(split), high / len(split)))
        factor_of = factor_of * jnp.repeat(draws, shape[axis_at] // shards_of).reshape([-1 if axis == axis_at else 1 for axis in range(len(shape))])
    return factor_of


def gaussian(rng, dims, spread, reach, shards=(), kind=jnp.bfloat16):
    entries = jax.random.normal(rng, dims, jnp.float32) * spread
    if len(shards) > 0:
        entries = levels(rng, dims, shards, -0.22, 0.18) * entries
    return jnp.clip(entries, min=-reach, max=reach).astype(kind)


def setup_inputs(seed: int = 0) -> dict:
    seeds = jax.random.split(jax.random.key(seed), 11)
    return {
        "queries": gaussian(seeds[0], (SEQS, LENGTH, HEADS * HD), 0.3, 1.75, ((1, 32), (2, 8))),
        "keys": gaussian(seeds[1], (SEQS, LENGTH, HEADS * HD), 0.3, 1.75, ((1, 32), (2, 8))),
        "values": gaussian(seeds[2], (SEQS, LENGTH, HEADS * HD), 1.0, 6.0, ((1, 32), (2, 8))),
        "gate_pre": gaussian(seeds[3], (SEQS, LENGTH, HEADS * HD), 1.5, 8.0, ((1, 32), (2, 8))),
        "grad_out": gaussian(seeds[4], (SEQS, LENGTH, D), 1.0, 6.0, ((1, 32), (2, 8))),
        "w_query": gaussian(seeds[5], (D, HEADS * HD), D ** -0.5, 0.09375, ((1, 8),)),
        "w_key": gaussian(seeds[6], (D, HEADS * HD), D ** -0.5, 0.09375, ((1, 8),)),
        "w_value": gaussian(seeds[7], (D, HEADS * HD), D ** -0.5, 0.09375, ((1, 8),)),
        "w_gate": gaussian(seeds[8], (D, HEADS * HD), D ** -0.5, 0.09375, ((1, 8),)),
        "w_out": gaussian(seeds[9], (HEADS * HD, D), (HEADS * HD) ** -0.5, 0.125, ((0, 8),)),
    }


def product(pattern, former, latter):
    return jnp.einsum(pattern, former.astype(jnp.float32), latter.astype(jnp.float32), precision=lax.Precision.HIGHEST)


def rounded(tensor):
    return lax.optimization_barrier(tensor.astype(jnp.bfloat16)).astype(jnp.float32)


def head_blocks(operands):
    queries, keys, values, d_output = operands
    factor = LENGTH ** -0.5
    causal = jnp.tril(jnp.ones((SPAN, SPAN), dtype=bool))
    key_state = product("snck,sncv->snkv", keys, values)
    query_state = product("snck,sncv->snkv", queries, d_output)
    zero_block = jnp.zeros_like(key_state[:, :1])
    prefix = jnp.concatenate([zero_block, jnp.cumsum(key_state, axis=1)[:, :-1]], axis=1)
    after = jnp.flip(jnp.cumsum(jnp.flip(query_state, 1), axis=1), 1)
    suffix = jnp.concatenate([after[:, 1:], zero_block], axis=1)
    scores = rounded(jnp.where(causal, product("sntk,snuk->sntu", queries, keys), 0.0))
    backward = rounded(jnp.where(causal, product("sntv,snuv->sntu", d_output, values), 0.0))
    attended = factor * (product("sntk,snkv->sntv", queries, prefix) + product("sntu,snuv->sntv", scores, values))
    d_query = factor * (product("sntv,snkv->sntk", d_output, prefix) + product("sntu,snuk->sntk", backward, keys))
    d_key = factor * (product("sntu,sntk->snuk", backward, queries) + product("snuv,snkv->snuk", values, suffix))
    d_value = factor * (product("sntu,sntv->snuv", scores, d_output) + product("snuk,snkv->snuv", keys, suffix))
    return attended, d_query.astype(jnp.bfloat16), d_key.astype(jnp.bfloat16), d_value.astype(jnp.bfloat16)


def reference(queries, keys, values, gate_pre, grad_out, w_query, w_key, w_value, w_gate, w_out):
    blocks = LENGTH // SPAN
    columns = HEADS * HD
    d_gated = jnp.dot(grad_out.reshape(SEQS * LENGTH, D), w_out.T, preferred_element_type=jnp.float32).reshape(SEQS, LENGTH, columns)
    gate_open = jax.nn.sigmoid(gate_pre.astype(jnp.float32))
    d_output = (d_gated * gate_open).astype(jnp.bfloat16)

    def to_heads(tensor):
        return jnp.transpose(tensor.reshape(SEQS, blocks, SPAN, HEADS, HD), (3, 0, 1, 2, 4))

    def from_heads(tensor):
        return jnp.transpose(tensor, (1, 2, 3, 0, 4)).reshape(SEQS, LENGTH, columns)

    results = lax.map(head_blocks, (to_heads(queries), to_heads(keys), to_heads(values), to_heads(d_output)))
    attended, d_query, d_key, d_value = [from_heads(stacked) for stacked in results]
    d_gate = (d_gated * attended * gate_open * (1.0 - gate_open)).astype(jnp.bfloat16)
    group_cols = columns // N_HEAD

    def by_group(tensor):
        return jnp.transpose(tensor.reshape(SEQS * LENGTH, N_HEAD, group_cols), (1, 0, 2))

    def weight_group(weight):
        return jnp.transpose(weight.reshape(D, N_HEAD, group_cols), (1, 2, 0))

    grads = tuple(by_group(tensor) for tensor in (d_query, d_key, d_value, d_gate))
    weights = tuple(weight_group(weight) for weight in (w_query, w_key, w_value, w_gate))

    def add_group(running, slices):
        grad_parts, weight_parts = slices
        partial_sum = jnp.zeros((SEQS * LENGTH, D), jnp.float32)
        for grad_part, weight_part in zip(grad_parts, weight_parts):
            partial_sum = partial_sum + jnp.dot(grad_part, weight_part, preferred_element_type=jnp.float32)
        return running + rounded(partial_sum), None

    total, unused = lax.scan(add_group, jnp.zeros((SEQS * LENGTH, D), jnp.float32), (grads, weights))
    return total.astype(jnp.bfloat16).reshape(SEQS, LENGTH, D)
```

```python
import jax
import jax.numpy as jnp
from jax import lax
from jax.experimental import pallas as pl
from jax.experimental.pallas import tpu as pltpu
from jax.sharding import PartitionSpec as P

HD = 128
VMEM_LIMIT = 32 * 1024 * 1024
RELATIVE = (0, -1, 1, 2)


def params():
    return pltpu.CompilerParams(vmem_limit_bytes=VMEM_LIMIT)


def cost(flops, moved):
    return pl.CostEstimate(flops=int(flops), bytes_accessed=int(moved), transcendentals=0)


def mm(a, b, over_a, over_b):
    return lax.dot_general(
        a, b, (((over_a,), (over_b,)), ((), ())), preferred_element_type=jnp.float32
    )


def nn(a, b):
    return mm(a, b, 1, 0)


def nt(a, b):
    return mm(a, b, 1, 1)


def tn(a, b):
    return mm(a, b, 0, 0)


def whole(shape):
    return pl.BlockSpec(shape, lambda *at: (0,) * len(shape))


def key_state_kernel(k_ref, v_ref, out_ref):
    for s in range(out_ref.shape[0]):
        for h in range(out_ref.shape[1]):
            cols = slice(h * HD, (h + 1) * HD)
            out_ref[s, h] = tn(k_ref[s, :, cols], v_ref[s, :, cols]).astype(out_ref.dtype)


def pick_kernel(table_ref, w_ref, out_ref):
    out_ref[0] = w_ref[...]


def gated_start_kernel(table_ref, g_ref, a0, a1, b0, b1, w_ref, wo_ref, mine_ref, other_ref):
    k = pl.program_id(0)

    @pl.when(k == 0)
    def _():
        for s in range(2):
            mine_ref[s] = nt(g_ref[s], w_ref[...])
            other_ref[s] = nt(g_ref[s], wo_ref[0])

    for at, pair in ((1, (a0, a1)), (2, (b0, b1))):

        @pl.when(k == at)
        def _(pair=pair):
            for s in range(2):
                mine_ref[s] += nt(pair[s][...], w_ref[...])
                other_ref[s] += nt(pair[s][...], wo_ref[0])


def gated_end_kernel(table_ref, mine_in, other_in, c0, c1, w_ref, wo_ref, mine_ref, other_ref):
    for s, piece in enumerate((c0, c1)):
        other_ref[s] = other_in[s] + nt(piece[...], wo_ref[0])
        mine_ref[s] = mine_in[s] + nt(piece[...], w_ref[...])


def gate_kernel(mine_ref, theirs_ref, gate_ref, q_ref, d_out_ref, slope_ref, state_ref):
    for s in range(2):
        d_gated = mine_ref[s] + theirs_ref[s]
        gate_open = jax.nn.sigmoid(gate_ref[s].astype(jnp.float32))
        d_output = d_gated * gate_open
        rounded = d_output.astype(jnp.bfloat16)
        d_out_ref[s] = rounded
        slope_ref[s] = d_output * (1.0 - gate_open)
        for h in range(state_ref.shape[1]):
            cols = slice(h * HD, (h + 1) * HD)
            state_ref[s, h] = tn(q_ref[s, :, cols], rounded[:, cols]).astype(state_ref.dtype)


def make_inner_kernel(factor):
    def inner_kernel(q_ref, k_ref, v_ref, d_out_ref, slope_ref, prefix_ref, dq_ref, dg_ref, dk_ref, dv_ref):
        q, k, v, d_out = q_ref[0], k_ref[0], v_ref[0], d_out_ref[0]
        prefix = prefix_ref[0, 0]
        rows = q.shape[0]
        causal = lax.broadcasted_iota(jnp.int32, (rows, rows), 0) >= lax.broadcasted_iota(
            jnp.int32, (rows, rows), 1
        )
        scores = jnp.where(causal, nt(q, k), 0.0).astype(jnp.bfloat16)
        backward = jnp.where(causal, nt(d_out, v), 0.0).astype(jnp.bfloat16)
        attended = factor * (nn(q, prefix) + nn(scores, v))
        dg_ref[0] = (slope_ref[0] * attended).astype(jnp.bfloat16)
        dq_ref[0] = (factor * (nt(d_out, prefix) + nn(backward, k))).astype(jnp.bfloat16)
        dk_ref[0] = tn(backward, q)
        dv_ref[0] = tn(scores, d_out)

    return inner_kernel


def make_project_kernel(factor):
    def project_kernel(
        table_ref, dq_ref, dg_ref, dk_part, dv_part, k_ref, v_ref, suffix_ref, wq, wk, wv, wg, out_ref, dk_sc, dv_sc
    ):
        seq_count, rows, columns = k_ref.shape

        @pl.when(pl.program_id(0) == 0)
        def _():
            for s in range(seq_count):
                for h in range(columns // HD):
                    cols = slice(h * HD, (h + 1) * HD)
                    suffix = suffix_ref[s, h]
                    dk_sc[s, :, cols] = (
                        factor * (dk_part[s, :, cols] + nt(v_ref[s, :, cols], suffix))
                    ).astype(jnp.bfloat16)
                    dv_sc[s, :, cols] = (
                        factor * (dv_part[s, :, cols] + nn(k_ref[s, :, cols], suffix))
                    ).astype(jnp.bfloat16)

        for s in range(seq_count):
            total = nt(dq_ref[s], wq[...]) + nt(dk_sc[s], wk[...])
            total = total + nt(dv_sc[s], wv[...]) + nt(dg_ref[s], wg[...])
            out_ref[0, s] = total.astype(jnp.bfloat16)

    return project_kernel


def across_seq(state, reverse):
    peers, here = lax.axis_size("seq"), lax.axis_index("seq")

    def swap(x, by):
        return lax.ppermute(x, "seq", [(i, i ^ by) for i in range(peers)])

    def counted(x, bit):
        take = (here & bit) == 0 if reverse else (here & bit) != 0
        return jnp.where(take, x.astype(jnp.float32), 0.0)

    total, entering = state, jnp.zeros(state.shape, jnp.float32)
    for bit in (1, 2, 4):
        theirs = swap(total, bit)
        entering = entering + counted(theirs, bit)
        total = (total.astype(jnp.float32) + theirs.astype(jnp.float32)).astype(jnp.bfloat16)
    swapped = [swap(total, by) for by in (8, 16, 24)]
    for theirs, bit in zip(swapped, (8, 16, 16)):
        entering = entering + counted(theirs, bit)
    return entering.astype(jnp.bfloat16)


def body(queries, keys, values, gate_pre, grad_out, w_query, w_key, w_value, w_gate, w_out):
    seq_count, rows, columns = queries.shape
    head_count = columns // HD
    features = grad_out.shape[2]
    peers = lax.axis_size("head")
    ring = peers // 2
    factor = (lax.axis_size("seq") * rows) ** (-0.5)
    bf16, f32 = jnp.bfloat16, jnp.float32
    state_shape = (seq_count, head_count, HD, HD)
    cube = (seq_count, rows, columns)

    here = lax.axis_index("head")
    y, lane = here // 2, here % 2
    places = jnp.arange(8, dtype=jnp.int32)
    offset = places % 4
    offset = jnp.where(offset == 1, ring - 1, jnp.where(offset == 2, 1, jnp.where(offset == 3, 2, 0)))
    table = 2 * ((y + offset) % ring) + jnp.where(places < 4, 1 - lane, lane)
    table = table.astype(jnp.int32)

    def along_y(x, by):
        return lax.ppermute(x, "head", [(i, (i + 2 * by) % peers) for i in range(peers)])

    def other_core(x):
        return lax.ppermute(x, "head", [(i, i ^ 1) for i in range(peers)])

    g0, g1 = grad_out[0], grad_out[1]
    a0 = along_y(g0, 1)
    b1 = along_y(g1, -1)
    a1 = along_y(g1, 1)
    b0 = along_y(g0, -1)
    c0 = along_y(a0, 1)
    c1 = along_y(b1, -1)

    w_pick = pl.pallas_call(
        pick_kernel,
        out_shape=jax.ShapeDtypeStruct((4, columns, features), bf16),
        grid_spec=pltpu.PrefetchScalarGridSpec(
            num_scalar_prefetch=1,
            grid=(4,),
            in_specs=[pl.BlockSpec((columns, features), lambda k, t: (0, t[k]))],
            out_specs=pl.BlockSpec((1, columns, features), lambda k, t: (k, 0, 0)),
        ),
        compiler_params=params(),
        cost_estimate=cost(0, 2 * 4 * columns * features * 2),
    )(table, w_out)
    w_theirs = other_core(w_pick)

    key_state = pl.pallas_call(
        key_state_kernel,
        out_shape=jax.ShapeDtypeStruct(state_shape, bf16),
        compiler_params=params(),
        cost_estimate=cost(2 * seq_count * rows * columns * HD, 4 * seq_count * rows * columns),
    )(keys, values)
    prefix = across_seq(key_state, False)

    flat = (rows, features)
    two = [jax.ShapeDtypeStruct(cube, f32)] * 2
    piece_flops = 4 * seq_count * rows * features * columns
    mine, other = pl.pallas_call(
        gated_start_kernel,
        out_shape=two,
        grid_spec=pltpu.PrefetchScalarGridSpec(
            num_scalar_prefetch=1,
            grid=(3,),
            in_specs=[whole(grad_out.shape)]
            + [whole(flat)] * 4
            + [
                pl.BlockSpec((columns, features), lambda k, t: (0, t[4 + k])),
                pl.BlockSpec((1, columns, features), lambda k, t: (k, 0, 0)),
            ],
            out_specs=[whole(cube)] * 2,
        ),
        compiler_params=params(),
        cost_estimate=cost(3 * piece_flops, 4 * 1024 * 1024),
    )(table, grad_out, a0, a1, b0, b1, w_out, w_theirs)
    mine, other = pl.pallas_call(
        gated_end_kernel,
        out_shape=two,
        grid_spec=pltpu.PrefetchScalarGridSpec(
            num_scalar_prefetch=1,
            grid=(1,),
            in_specs=[whole(cube)] * 2
            + [whole(flat)] * 2
            + [
                pl.BlockSpec((columns, features), lambda k, t: (0, t[7])),
                pl.BlockSpec((1, columns, features), lambda k, t: (3, 0, 0)),
            ],
            out_specs=[whole(cube)] * 2,
        ),
        compiler_params=params(),
        cost_estimate=cost(piece_flops, 3 * 1024 * 1024),
    )(table, mine, other, c0, c1, w_out, w_theirs)
    theirs = other_core(other)

    d_output, slope, query_state = pl.pallas_call(
        gate_kernel,
        out_shape=[
            jax.ShapeDtypeStruct(cube, bf16),
            jax.ShapeDtypeStruct(cube, f32),
            jax.ShapeDtypeStruct(state_shape, bf16),
        ],
        compiler_params=params(),
        cost_estimate=cost(2 * seq_count * rows * columns * HD, 3 * 1024 * 1024),
    )(mine, theirs, gate_pre, queries)
    suffix = across_seq(query_state, True)

    block = pl.BlockSpec((1, rows, HD), lambda s, h: (s, 0, h))
    d_query, d_gate, dk_part, dv_part = pl.pallas_call(
        make_inner_kernel(factor),
        out_shape=[jax.ShapeDtypeStruct(cube, kind) for kind in (bf16, bf16, f32, f32)],
        grid=(seq_count, head_count),
        in_specs=[block] * 5 + [pl.BlockSpec((1, 1, HD, HD), lambda s, h: (s, h, 0, 0))],
        out_specs=[block] * 4,
        compiler_params=params(),
        cost_estimate=cost(12 * seq_count * rows * rows * columns, 3 * 1024 * 1024),
    )(queries, keys, values, d_output, slope, prefix)

    def project(first):
        weight = pl.BlockSpec((features, columns), lambda k, t: (t[first + k], 0))
        return pl.pallas_call(
            make_project_kernel(factor),
            out_shape=jax.ShapeDtypeStruct((4, seq_count, rows, features), bf16),
            grid_spec=pltpu.PrefetchScalarGridSpec(
                num_scalar_prefetch=1,
                grid=(4,),
                in_specs=[whole(cube)] * 6 + [whole(state_shape)] + [weight] * 4,
                out_specs=pl.BlockSpec((1, seq_count, rows, features), lambda k, t: (k, 0, 0, 0)),
                scratch_shapes=[pltpu.VMEM(cube, bf16)] * 2,
            ),
            compiler_params=params(),
            cost_estimate=cost(32 * seq_count * rows * columns * features, 8 * 1024 * 1024),
        )(table, d_query, d_gate, dk_part, dv_part, keys, values, suffix, w_query, w_key, w_value, w_gate)

    theirs = other_core(project(0))
    own = project(4)

    def chip(place, s):
        return own[place, s].astype(f32) + theirs[place, s].astype(f32)

    up_far = along_y(chip(3, 0).astype(bf16), 1)
    down_far = along_y(chip(3, 1).astype(bf16), -1)
    up_near = along_y(chip(2, 1).astype(bf16), 1)
    down_near = along_y(chip(1, 0).astype(bf16), -1)
    up_last = along_y((chip(2, 0) + up_far.astype(f32)).astype(bf16), 1)
    down_last = along_y((chip(1, 1) + down_far.astype(f32)).astype(bf16), -1)
    out0 = chip(0, 0) + down_near.astype(f32) + up_last.astype(f32)
    out1 = chip(0, 1) + up_near.astype(f32) + down_last.astype(f32)
    return jnp.stack([out0, out1]).astype(bf16)


def solution(mesh):
    tokens = P(None, "seq", "head")
    return jax.shard_map(
        body,
        mesh=mesh,
        in_specs=(tokens,) * 5 + (P(None, "head"),) * 4 + (P("head", None),),
        out_specs=tokens,
        check_vma=False,
    )
```

```python
import jax
import jax.numpy as jnp
from jax import lax
from jax.experimental import pallas as pl
from jax.experimental.pallas import tpu as pltpu
from jax.sharding import PartitionSpec as P

HD = 128
MIB = 1024 * 1024
RELATIVE = (0, -1, 1, 2)


def params(mib=8):
    return pltpu.CompilerParams(vmem_limit_bytes=mib * MIB)


def cost(flops, moved):
    return pl.CostEstimate(flops=int(flops), bytes_accessed=int(moved), transcendentals=0)


def mm(a, b, over_a, over_b):
    return lax.dot_general(
        a, b, (((over_a,), (over_b,)), ((), ())), preferred_element_type=jnp.float32
    )


def nn(a, b):
    return mm(a, b, 1, 0)


def nt(a, b):
    return mm(a, b, 1, 1)


def tn(a, b):
    return mm(a, b, 0, 0)


def whole(shape):
    return pl.BlockSpec(shape, lambda *at: (0,) * len(shape))


def key_state_kernel(k_ref, v_ref, out_ref):
    for s in range(out_ref.shape[0]):
        for h in range(out_ref.shape[1]):
            cols = slice(h * HD, (h + 1) * HD)
            out_ref[s, h] = tn(k_ref[s, :, cols], v_ref[s, :, cols]).astype(out_ref.dtype)


def pick_kernel(table_ref, w_ref, theirs_ref, own_ref, sems):
    copies = []
    for k in range(8):
        out_ref = theirs_ref if k < 4 else own_ref
        features = out_ref.shape[2]
        cols = pl.ds(pl.multiple_of(table_ref[k] * features, features), features)
        copies.append(pltpu.make_async_copy(w_ref.at[:, cols], out_ref.at[k % 4], sems.at[k]))
        copies[-1].start()
    for copy in copies:
        copy.wait()


def gated_start_kernel(g_ref, a0, a1, b0, b1, w_ref, wo_ref, mine_ref, other_ref):
    k = pl.program_id(0)

    @pl.when(k == 0)
    def _():
        for s in range(2):
            mine_ref[s] = nt(g_ref[s], w_ref[0])
            other_ref[s] = nt(g_ref[s], wo_ref[0])

    for at, pair in ((1, (a0, a1)), (2, (b0, b1))):

        @pl.when(k == at)
        def _(pair=pair):
            for s in range(2):
                mine_ref[s] += nt(pair[s][...], w_ref[0])
                other_ref[s] += nt(pair[s][...], wo_ref[0])


def gated_end_kernel(mine_in, other_in, c0, c1, w_ref, wo_ref, mine_ref, other_ref):
    for s, piece in enumerate((c0, c1)):
        other_ref[s] = other_in[s] + nt(piece[...], wo_ref[0])
        mine_ref[s] = mine_in[s] + nt(piece[...], w_ref[0])


def gate_kernel(mine_ref, theirs_ref, gate_ref, q_ref, d_out_ref, slope_ref, state_ref):
    for s in range(2):
        d_gated = mine_ref[s] + theirs_ref[s]
        gate_open = jax.nn.sigmoid(gate_ref[s].astype(jnp.float32))
        d_output = d_gated * gate_open
        rounded = d_output.astype(jnp.bfloat16)
        d_out_ref[s] = rounded
        slope_ref[s] = d_output * (1.0 - gate_open)
        for h in range(state_ref.shape[1]):
            cols = slice(h * HD, (h + 1) * HD)
            state_ref[s, h] = tn(q_ref[s, :, cols], rounded[:, cols]).astype(state_ref.dtype)


def make_inner_kernel(factor):
    def inner_kernel(q_ref, k_ref, v_ref, d_out_ref, slope_ref, prefix_ref, dq_ref, dg_ref, dk_ref, dv_ref):
        q, k, v, d_out = q_ref[0], k_ref[0], v_ref[0], d_out_ref[0]
        prefix = prefix_ref[0, 0]
        rows = q.shape[0]
        causal = lax.broadcasted_iota(jnp.int32, (rows, rows), 0) >= lax.broadcasted_iota(
            jnp.int32, (rows, rows), 1
        )
        scores = jnp.where(causal, nt(q, k), 0.0).astype(jnp.bfloat16)
        backward = jnp.where(causal, nt(d_out, v), 0.0).astype(jnp.bfloat16)
        attended = factor * (nn(q, prefix) + nn(scores, v))
        dg_ref[0] = (slope_ref[0] * attended).astype(jnp.bfloat16)
        dq_ref[0] = (factor * (nt(d_out, prefix) + nn(backward, k))).astype(jnp.bfloat16)
        dk_ref[0] = tn(backward, q)
        dv_ref[0] = tn(scores, d_out)

    return inner_kernel


def make_project_kernel(factor, first):
    def project_kernel(
        table_ref, dq_ref, dg_ref, dk_part, dv_part, k_ref, v_ref, suffix_ref,
        wq, wk, wv, wg, out_ref, dk_sc, dv_sc, held, sems,
    ):
        seq_count, rows, columns = k_ref.shape
        features = out_ref.shape[3]
        here = pl.program_id(0)

        def copies(k):
            at = pl.ds(pl.multiple_of(table_ref[first + k] * features, features), features)
            return [
                pltpu.make_async_copy(weight.at[at, :], held.at[k, i], sems.at[k, i])
                for i, weight in enumerate((wq, wk, wv, wg))
            ]

        @pl.when(here == 0)
        def _():
            for k in range(4):
                for copy in copies(k):
                    copy.start()

        @pl.when(pl.program_id(0) == 0)
        def _():
            for s in range(seq_count):
                for h in range(columns // HD):
                    cols = slice(h * HD, (h + 1) * HD)
                    suffix = suffix_ref[s, h]
                    dk_sc[s, :, cols] = (
                        factor * (dk_part[s, :, cols] + nt(v_ref[s, :, cols], suffix))
                    ).astype(jnp.bfloat16)
                    dv_sc[s, :, cols] = (
                        factor * (dv_part[s, :, cols] + nn(k_ref[s, :, cols], suffix))
                    ).astype(jnp.bfloat16)

        for copy in copies(here):
            copy.wait()
        for s in range(seq_count):
            total = nt(dq_ref[s], held[here, 0]) + nt(dk_sc[s], held[here, 1])
            total = total + nt(dv_sc[s], held[here, 2]) + nt(dg_ref[s], held[here, 3])
            out_ref[0, s] = total.astype(jnp.bfloat16)

    return project_kernel


def together(*arrays):
    return lax.optimization_barrier(arrays)


def swap(x, by):
    return lax.ppermute(x, "seq", [(i, i ^ by) for i in range(lax.axis_size("seq"))])


def counted(x, bit, reverse):
    here = lax.axis_index("seq")
    take = (here & bit) == 0 if reverse else (here & bit) != 0
    return jnp.where(take, x.astype(jnp.float32), 0.0)


def joined(total, theirs):
    return (total.astype(jnp.float32) + theirs.astype(jnp.float32)).astype(jnp.bfloat16)


def entering(received, reverse):
    total = 0.0
    for theirs, bit in zip(received, (1, 2, 4, 8, 16, 16)):
        total = total + counted(theirs, bit, reverse)
    return total.astype(jnp.bfloat16)


def make_sum_kernel(counts):
    def sum_kernel(*refs):
        terms, outs = refs[: sum(counts)], refs[sum(counts) :]
        first = 0
        for at, count in enumerate(counts):
            total = terms[first][...].astype(jnp.float32).reshape(terms[first].shape[-2:])
            for term in terms[first + 1 : first + count]:
                total = total + term[...].astype(jnp.float32).reshape(total.shape)
            if len(outs) == len(counts):
                outs[at][...] = total.astype(jnp.bfloat16)
            else:
                outs[0][at] = total.astype(jnp.bfloat16)
            first += count

    return sum_kernel


def sums(groups, shape, stacked=False):
    arrays, specs = [], []
    for group in groups:
        for term in group:
            if isinstance(term, tuple):
                array, place, s = term
                arrays.append(array)
                specs.append(pl.BlockSpec((1, 1) + shape, lambda i, at=(place, s): at + (0, 0)))
            else:
                arrays.append(term)
                specs.append(whole(shape))
    if stacked:
        outs = jax.ShapeDtypeStruct((len(groups),) + shape, jnp.bfloat16)
        out_specs = whole(outs.shape)
    else:
        outs = [jax.ShapeDtypeStruct(shape, jnp.bfloat16)] * len(groups)
        out_specs = [whole(shape)] * len(groups)
    return pl.pallas_call(
        make_sum_kernel([len(group) for group in groups]),
        out_shape=outs,
        grid=(1,),
        in_specs=specs,
        out_specs=out_specs,
        compiler_params=params(),
        cost_estimate=cost(0, (len(arrays) + len(groups)) * shape[0] * shape[1] * 2),
    )(*arrays)


def body(queries, keys, values, gate_pre, grad_out, w_query, w_key, w_value, w_gate, w_out):
    seq_count, rows, columns = queries.shape
    head_count = columns // HD
    features = grad_out.shape[2]
    peers = lax.axis_size("head")
    ring = peers // 2
    factor = (lax.axis_size("seq") * rows) ** (-0.5)
    bf16, f32 = jnp.bfloat16, jnp.float32
    state_shape = (seq_count, head_count, HD, HD)
    cube = (seq_count, rows, columns)

    here = lax.axis_index("head")
    y, lane = here // 2, here % 2
    places = jnp.arange(8, dtype=jnp.int32)
    offset = places % 4
    offset = jnp.where(offset == 1, ring - 1, jnp.where(offset == 2, 1, jnp.where(offset == 3, 2, 0)))
    table = 2 * ((y + offset) % ring) + jnp.where(places < 4, 1 - lane, lane)
    table = table.astype(jnp.int32)

    def along_y(x, by):
        return lax.ppermute(x, "head", [(i, (i + 2 * by) % peers) for i in range(peers)])

    def other_core(x):
        return lax.ppermute(x, "head", [(i, i ^ 1) for i in range(peers)])

    g0, g1 = grad_out[0], grad_out[1]
    a0 = along_y(g0, 1)
    b1 = along_y(g1, -1)
    a1 = along_y(g1, 1)
    b0 = along_y(g0, -1)

    total = pl.pallas_call(
        key_state_kernel,
        out_shape=jax.ShapeDtypeStruct(state_shape, bf16),
        compiler_params=params(),
        cost_estimate=cost(2 * seq_count * rows * columns * HD, 4 * seq_count * rows * columns),
    )(keys, values)
    seq_peers = lax.axis_size("seq")
    rows_of = [[x * 8 + z for z in range(8)] for x in range(seq_peers // 8)]
    line = lax.all_gather(total, "seq", axis_index_groups=rows_of)
    c0 = along_y(a0, 1)
    c1 = along_y(b1, -1)

    w_pick, w_own = pl.pallas_call(
        pick_kernel,
        out_shape=[jax.ShapeDtypeStruct((4, columns, features), bf16)] * 2,
        grid_spec=pltpu.PrefetchScalarGridSpec(
            num_scalar_prefetch=1,
            grid=(1,),
            in_specs=[pl.BlockSpec(memory_space=pltpu.HBM)],
            out_specs=[whole((4, columns, features))] * 2,
            scratch_shapes=[pltpu.SemaphoreType.DMA((8,))],
        ),
        compiler_params=params(),
        cost_estimate=cost(0, 2 * 8 * columns * features * 2),
    )(table, w_out)
    w_theirs = other_core(w_pick)

    flat = (rows, features)
    two = [jax.ShapeDtypeStruct(cube, f32)] * 2
    piece_flops = 4 * seq_count * rows * features * columns
    piece = pl.BlockSpec((1, columns, features), lambda k: (k, 0, 0))
    mine, other = pl.pallas_call(
        gated_start_kernel,
        out_shape=two,
        grid=(3,),
        in_specs=[whole(grad_out.shape)] + [whole(flat)] * 4 + [piece] * 2,
        out_specs=[whole(cube)] * 2,
        compiler_params=params(),
        cost_estimate=cost(3 * piece_flops, 4 * MIB),
    )(grad_out, a0, a1, b0, b1, w_own, w_theirs)
    piece = pl.BlockSpec((1, columns, features), lambda k: (3, 0, 0))
    mine, other = pl.pallas_call(
        gated_end_kernel,
        out_shape=two,
        grid=(1,),
        in_specs=[whole(cube)] * 2 + [whole(flat)] * 2 + [piece] * 2,
        out_specs=[whole(cube)] * 2,
        compiler_params=params(),
        cost_estimate=cost(piece_flops, 3 * MIB),
    )(mine, other, c0, c1, w_own, w_theirs)
    theirs = other_core(other)

    d_output, slope, query_state = pl.pallas_call(
        gate_kernel,
        out_shape=[
            jax.ShapeDtypeStruct(cube, bf16),
            jax.ShapeDtypeStruct(cube, f32),
            jax.ShapeDtypeStruct(state_shape, bf16),
        ],
        compiler_params=params(),
        cost_estimate=cost(2 * seq_count * rows * columns * HD, 3 * 1024 * 1024),
    )(mine, theirs, gate_pre, queries)
    after = [swap(query_state, 1)]
    line, after[0] = together(line, after[0])
    z = lax.axis_index("seq") % 8
    earlier = (jnp.arange(8) < z).reshape(8, 1, 1, 1, 1)
    line = line.astype(f32)
    prefix = jnp.where(earlier, line, 0.0).sum(0)
    row_total = line.sum(0).astype(bf16)
    for by, bit in ((8, 8), (16, 16), (24, 16)):
        prefix = prefix + counted(swap(row_total, by), bit, False)
    prefix = prefix.astype(bf16)
    total = joined(query_state, after[0])
    after.append(swap(total, 2))

    block = pl.BlockSpec((1, rows, HD), lambda s, h: (s, 0, h))
    d_query, d_gate, dk_part, dv_part = pl.pallas_call(
        make_inner_kernel(factor),
        out_shape=[jax.ShapeDtypeStruct(cube, kind) for kind in (bf16, bf16, f32, f32)],
        grid=(seq_count, head_count),
        in_specs=[block] * 5 + [pl.BlockSpec((1, 1, HD, HD), lambda s, h: (s, h, 0, 0))],
        out_specs=[block] * 4,
        compiler_params=params(),
        cost_estimate=cost(12 * seq_count * rows * rows * columns, 3 * 1024 * 1024),
    )(queries, keys, values, d_output, slope, prefix)

    after[1], d_query = together(after[1], d_query)
    total = joined(total, after[1])
    after.append(swap(total, 4))
    total = joined(total, after[2])
    after += [swap(total, by) for by in (8, 16, 24)]
    suffix = entering(after, True)

    def project(first):
        weight = pl.BlockSpec(memory_space=pltpu.HBM)
        return pl.pallas_call(
            make_project_kernel(factor, first),
            out_shape=jax.ShapeDtypeStruct((4, seq_count, rows, features), bf16),
            grid_spec=pltpu.PrefetchScalarGridSpec(
                num_scalar_prefetch=1,
                grid=(4,),
                in_specs=[whole(cube)] * 6 + [whole(state_shape)] + [weight] * 4,
                out_specs=pl.BlockSpec((1, seq_count, rows, features), lambda k, t: (k, 0, 0, 0)),
                scratch_shapes=[pltpu.VMEM(cube, bf16)] * 2
                + [pltpu.VMEM((4, 4, features, columns), bf16), pltpu.SemaphoreType.DMA((4, 4))],
            ),
            compiler_params=params(16),
            cost_estimate=cost(32 * seq_count * rows * columns * features, 8 * 1024 * 1024),
        )(table, d_query, d_gate, dk_part, dv_part, keys, values, suffix, w_query, w_key, w_value, w_gate)

    theirs = other_core(project(0))
    own = project(4)

    def chip(place, s):
        return [(own, place, s), (theirs, place, s)]

    far0, far1 = sums([chip(3, 0), chip(3, 1)], flat)
    up_far = along_y(far0, 1)
    down_far = along_y(far1, -1)
    near1, near0 = sums([chip(2, 1), chip(1, 0)], flat)
    up_near = along_y(near1, 1)
    down_near = along_y(near0, -1)
    (last0,) = sums([chip(2, 0) + [up_far]], flat)
    (last1,) = sums([chip(1, 1) + [down_far]], flat)
    up_last = along_y(last0, 1)
    down_last = along_y(last1, -1)
    return sums([chip(0, 0) + [down_near, up_last], chip(0, 1) + [up_near, down_last]], flat, stacked=True)


def solution(mesh):
    tokens = P(None, "seq", "head")
    return jax.shard_map(
        body,
        mesh=mesh,
        in_specs=(tokens,) * 5 + (P(None, "head"),) * 4 + (P("head", None),),
        out_specs=tokens,
        check_vma=False,
    )
```

```python
import jax
import jax.numpy as jnp
from jax import lax
from jax.experimental import pallas as pl
from jax.experimental.pallas import tpu as pltpu
from jax.sharding import PartitionSpec as P

HD = 128
PROJ = 48
PICK = 54
INNER = 48
SUM = 8
GATE = 8
MIB = 1024 * 1024
RELATIVE = (0, -1, 1, 2)


def params(mib=8):
    return pltpu.CompilerParams(vmem_limit_bytes=mib * MIB)


def cost(flops, moved):
    return pl.CostEstimate(flops=int(flops), bytes_accessed=int(moved), transcendentals=0)


def mm(a, b, over_a, over_b):
    return lax.dot_general(
        a, b, (((over_a,), (over_b,)), ((), ())), preferred_element_type=jnp.float32
    )


def nn(a, b):
    return mm(a, b, 1, 0)


def nt(a, b):
    return mm(a, b, 1, 1)


def tn(a, b):
    return mm(a, b, 0, 0)


def whole(shape):
    return pl.BlockSpec(shape, lambda *at: (0,) * len(shape))


def key_state_kernel(k_ref, v_ref, out_ref):
    for s in range(out_ref.shape[0]):
        for h in range(out_ref.shape[1]):
            cols = slice(h * HD, (h + 1) * HD)
            out_ref[s, h] = tn(k_ref[s, :, cols], v_ref[s, :, cols]).astype(out_ref.dtype)


def pick_kernel(table_ref, w_ref, theirs_ref, own_ref, sems):
    copies = []
    for k in range(8):
        out_ref = theirs_ref if k < 4 else own_ref
        features = out_ref.shape[2]
        cols = pl.ds(pl.multiple_of(table_ref[k] * features, features), features)
        copies.append(pltpu.make_async_copy(w_ref.at[:, cols], out_ref.at[k % 4], sems.at[k]))
        copies[-1].start()
    for copy in copies:
        copy.wait()


def gated_start_kernel(g_ref, a_ref, b_ref, w_ref, wo_ref, mine_ref, other_ref):
    k = pl.program_id(0)

    @pl.when(k == 0)
    def _():
        for s in range(2):
            mine_ref[s] = nt(g_ref[s], w_ref[0])
            other_ref[s] = nt(g_ref[s], wo_ref[0])

    for at, piece in ((1, a_ref), (2, b_ref)):

        @pl.when(k == at)
        def _(piece=piece):
            for s in range(2):
                mine_ref[s] += nt(piece[s], w_ref[0])
                other_ref[s] += nt(piece[s], wo_ref[0])


def gated_end_kernel(mine_in, other_in, c0, c1, w_ref, wo_ref, mine_ref, other_ref):
    for s, piece in enumerate((c0, c1)):
        other_ref[s] = other_in[s] + nt(piece[...], wo_ref[0])
        mine_ref[s] = mine_in[s] + nt(piece[...], w_ref[0])


def gate_kernel(mine_ref, theirs_ref, gate_ref, q_ref, d_out_ref, slope_ref, state_ref):
    for s in range(2):
        d_gated = mine_ref[s] + theirs_ref[s]
        gate_open = jax.nn.sigmoid(gate_ref[s].astype(jnp.float32))
        d_output = d_gated * gate_open
        rounded = d_output.astype(jnp.bfloat16)
        d_out_ref[s] = rounded
        slope_ref[s] = d_output * (1.0 - gate_open)
        for h in range(state_ref.shape[1]):
            cols = slice(h * HD, (h + 1) * HD)
            state_ref[s, h] = tn(q_ref[s, :, cols], rounded[:, cols]).astype(state_ref.dtype)


def make_inner_kernel(factor):
    def inner_kernel(q_ref, k_ref, v_ref, d_out_ref, slope_ref, prefix_ref, dq_ref, dg_ref, dk_ref, dv_ref):
        q, k, v, d_out = q_ref[0], k_ref[0], v_ref[0], d_out_ref[0]
        prefix = prefix_ref[0, 0]
        rows = q.shape[0]
        causal = lax.broadcasted_iota(jnp.int32, (rows, rows), 0) >= lax.broadcasted_iota(
            jnp.int32, (rows, rows), 1
        )
        scores = jnp.where(causal, nt(q, k), 0.0).astype(jnp.bfloat16)
        backward = jnp.where(causal, nt(d_out, v), 0.0).astype(jnp.bfloat16)
        attended = factor * (nn(q, prefix) + nn(scores, v))
        dg_ref[0] = (slope_ref[0] * attended).astype(jnp.bfloat16)
        dq_ref[0] = (factor * (nt(d_out, prefix) + nn(backward, k))).astype(jnp.bfloat16)
        dk_ref[0] = tn(backward, q)
        dv_ref[0] = tn(scores, d_out)

    return inner_kernel


def make_project_kernel(factor, first):
    def project_kernel(
        table_ref, dq_ref, dg_ref, dk_part, dv_part, k_ref, v_ref, suffix_ref,
        wq, wk, wv, wg, out_ref, dk_sc, dv_sc, held, sems,
    ):
        seq_count, rows, columns = k_ref.shape
        features = out_ref.shape[3]
        here = pl.program_id(0)

        def copies(k):
            at = pl.ds(pl.multiple_of(table_ref[first + k] * features, features), features)
            return [
                pltpu.make_async_copy(weight.at[at, :], held.at[k, i], sems.at[k, i])
                for i, weight in enumerate((wq, wk, wv, wg))
            ]

        @pl.when(here == 0)
        def _():
            for k in range(4):
                for copy in copies(k):
                    copy.start()

        @pl.when(pl.program_id(0) == 0)
        def _():
            for s in range(seq_count):
                for h in range(columns // HD):
                    cols = slice(h * HD, (h + 1) * HD)
                    suffix = suffix_ref[s, h]
                    dk_sc[s, :, cols] = (
                        factor * (dk_part[s, :, cols] + nt(v_ref[s, :, cols], suffix))
                    ).astype(jnp.bfloat16)
                    dv_sc[s, :, cols] = (
                        factor * (dv_part[s, :, cols] + nn(k_ref[s, :, cols], suffix))
                    ).astype(jnp.bfloat16)

        for copy in copies(here):
            copy.wait()
        for s in range(seq_count):
            total = nt(dq_ref[s], held[here, 0]) + nt(dk_sc[s], held[here, 1])
            total = total + nt(dv_sc[s], held[here, 2]) + nt(dg_ref[s], held[here, 3])
            out_ref[0, s] = total.astype(jnp.bfloat16)

    return project_kernel


def together(*arrays):
    return lax.optimization_barrier(arrays)


def swap(x, by):
    return lax.ppermute(x, "seq", [(i, i ^ by) for i in range(lax.axis_size("seq"))])


def counted(x, bit, reverse):
    here = lax.axis_index("seq")
    take = (here & bit) == 0 if reverse else (here & bit) != 0
    return jnp.where(take, x.astype(jnp.float32), 0.0)


def joined(total, theirs):
    return (total.astype(jnp.float32) + theirs.astype(jnp.float32)).astype(jnp.bfloat16)


def entering(received, reverse):
    total = 0.0
    for theirs, bit in zip(received, (1, 2, 4, 8, 16, 16)):
        total = total + counted(theirs, bit, reverse)
    return total.astype(jnp.bfloat16)


def make_sum_kernel(counts):
    def sum_kernel(*refs):
        terms, outs = refs[: sum(counts)], refs[sum(counts) :]
        first = 0
        for at, count in enumerate(counts):
            total = terms[first][...].astype(jnp.float32).reshape(terms[first].shape[-2:])
            for term in terms[first + 1 : first + count]:
                total = total + term[...].astype(jnp.float32).reshape(total.shape)
            if len(outs) == len(counts):
                outs[at][...] = total.astype(jnp.bfloat16)
            else:
                outs[0][at] = total.astype(jnp.bfloat16)
            first += count

    return sum_kernel


def sums(groups, shape, stacked=False):
    arrays, specs = [], []
    for group in groups:
        for term in group:
            if isinstance(term, tuple):
                array, place, s = term
                arrays.append(array)
                specs.append(pl.BlockSpec((1, 1) + shape, lambda i, at=(place, s): at + (0, 0)))
            else:
                arrays.append(term)
                specs.append(whole(shape))
    if stacked:
        outs = jax.ShapeDtypeStruct((len(groups),) + shape, jnp.bfloat16)
        out_specs = whole(outs.shape)
    else:
        outs = [jax.ShapeDtypeStruct(shape, jnp.bfloat16)] * len(groups)
        out_specs = [whole(shape)] * len(groups)
    return pl.pallas_call(
        make_sum_kernel([len(group) for group in groups]),
        out_shape=outs,
        grid=(1,),
        in_specs=specs,
        out_specs=out_specs,
        compiler_params=params(SUM),
        cost_estimate=cost(0, (len(arrays) + len(groups)) * shape[0] * shape[1] * 2),
    )(*arrays)


def body(queries, keys, values, gate_pre, grad_out, w_query, w_key, w_value, w_gate, w_out):
    seq_count, rows, columns = queries.shape
    head_count = columns // HD
    features = grad_out.shape[2]
    peers = lax.axis_size("head")
    ring = peers // 2
    factor = (lax.axis_size("seq") * rows) ** (-0.5)
    bf16, f32 = jnp.bfloat16, jnp.float32
    state_shape = (seq_count, head_count, HD, HD)
    cube = (seq_count, rows, columns)

    here = lax.axis_index("head")
    y, lane = here // 2, here % 2
    places = jnp.arange(8, dtype=jnp.int32)
    offset = places % 4
    offset = jnp.where(offset == 1, ring - 1, jnp.where(offset == 2, 1, jnp.where(offset == 3, 2, 0)))
    table = 2 * ((y + offset) % ring) + jnp.where(places < 4, 1 - lane, lane)
    table = table.astype(jnp.int32)

    def along_y(x, by):
        return lax.ppermute(x, "head", [(i, (i + 2 * by) % peers) for i in range(peers)])

    def other_core(x):
        return lax.ppermute(x, "head", [(i, i ^ 1) for i in range(peers)])

    a = along_y(grad_out, 1)
    b = along_y(grad_out, -1)
    c0 = along_y(a[0], 1)
    c1 = along_y(b[1], -1)

    total = pl.pallas_call(
        key_state_kernel,
        out_shape=jax.ShapeDtypeStruct(state_shape, bf16),
        compiler_params=params(),
        cost_estimate=cost(2 * seq_count * rows * columns * HD, 4 * seq_count * rows * columns),
    )(keys, values)
    before = [swap(total, 1)]
    total = joined(total, before[0])
    a, total = together(a, total)
    before.append(swap(total, 2))

    w_pick, w_own = pl.pallas_call(
        pick_kernel,
        out_shape=[jax.ShapeDtypeStruct((4, columns, features), bf16)] * 2,
        grid_spec=pltpu.PrefetchScalarGridSpec(
            num_scalar_prefetch=1,
            grid=(1,),
            in_specs=[pl.BlockSpec(memory_space=pltpu.HBM)],
            out_specs=[whole((4, columns, features))] * 2,
            scratch_shapes=[pltpu.SemaphoreType.DMA((8,))],
        ),
        compiler_params=params(PICK),
        cost_estimate=cost(0, 2 * 8 * columns * features * 2),
    )(table, w_out)
    w_theirs = other_core(w_pick)

    flat = (rows, features)
    two = [jax.ShapeDtypeStruct(cube, f32)] * 2
    piece_flops = 4 * seq_count * rows * features * columns
    piece = pl.BlockSpec((1, columns, features), lambda k: (k, 0, 0))
    mine, other = pl.pallas_call(
        gated_start_kernel,
        out_shape=two,
        grid=(3,),
        in_specs=[whole(grad_out.shape)] * 3 + [piece] * 2,
        out_specs=[whole(cube)] * 2,
        compiler_params=params(),
        cost_estimate=cost(3 * piece_flops, 4 * MIB),
    )(grad_out, a, b, w_own, w_theirs)
    piece = pl.BlockSpec((1, columns, features), lambda k: (3, 0, 0))
    mine, other = pl.pallas_call(
        gated_end_kernel,
        out_shape=two,
        grid=(1,),
        in_specs=[whole(cube)] * 2 + [whole(flat)] * 2 + [piece] * 2,
        out_specs=[whole(cube)] * 2,
        compiler_params=params(),
        cost_estimate=cost(piece_flops, 3 * MIB),
    )(mine, other, c0, c1, w_own, w_theirs)
    other, before[1] = together(other, before[1])
    theirs = other_core(other)
    total = joined(total, before[1])
    before.append(swap(total, 4))

    d_output, slope, query_state = pl.pallas_call(
        gate_kernel,
        out_shape=[
            jax.ShapeDtypeStruct(cube, bf16),
            jax.ShapeDtypeStruct(cube, f32),
            jax.ShapeDtypeStruct(state_shape, bf16),
        ],
        compiler_params=params(GATE),
        cost_estimate=cost(2 * seq_count * rows * columns * HD, 3 * 1024 * 1024),
    )(mine, theirs, gate_pre, queries)
    after = [swap(query_state, 1)]
    after[0], before[2] = together(after[0], before[2])
    total = joined(total, before[2])
    before += [swap(total, by) for by in (8, 16, 24)]
    prefix = entering(before, False)
    total = joined(query_state, after[0])
    after.append(swap(total, 2))

    block = pl.BlockSpec((1, rows, HD), lambda s, h: (s, 0, h))
    d_query, d_gate, dk_part, dv_part = pl.pallas_call(
        make_inner_kernel(factor),
        out_shape=[jax.ShapeDtypeStruct(cube, kind) for kind in (bf16, bf16, f32, f32)],
        grid=(seq_count, head_count),
        in_specs=[block] * 5 + [pl.BlockSpec((1, 1, HD, HD), lambda s, h: (s, h, 0, 0))],
        out_specs=[block] * 4,
        compiler_params=params(INNER),
        cost_estimate=cost(12 * seq_count * rows * rows * columns, 3 * 1024 * 1024),
    )(queries, keys, values, d_output, slope, prefix)

    after[1], d_query = together(after[1], d_query)
    total = joined(total, after[1])
    after.append(swap(total, 4))
    total = joined(total, after[2])
    after += [swap(total, by) for by in (8, 16, 24)]
    suffix = entering(after, True)

    def project(first):
        weight = pl.BlockSpec(memory_space=pltpu.HBM)
        return pl.pallas_call(
            make_project_kernel(factor, first),
            out_shape=jax.ShapeDtypeStruct((4, seq_count, rows, features), bf16),
            grid_spec=pltpu.PrefetchScalarGridSpec(
                num_scalar_prefetch=1,
                grid=(4,),
                in_specs=[whole(cube)] * 6 + [whole(state_shape)] + [weight] * 4,
                out_specs=pl.BlockSpec((1, seq_count, rows, features), lambda k, t: (k, 0, 0, 0)),
                scratch_shapes=[pltpu.VMEM(cube, bf16)] * 2
                + [pltpu.VMEM((4, 4, features, columns), bf16), pltpu.SemaphoreType.DMA((4, 4))],
            ),
            compiler_params=params(PROJ),
            cost_estimate=cost(32 * seq_count * rows * columns * features, 8 * 1024 * 1024),
        )(table, d_query, d_gate, dk_part, dv_part, keys, values, suffix, w_query, w_key, w_value, w_gate)

    theirs = other_core(project(0))
    own = project(4)

    def chip(place, s):
        return [(own, place, s), (theirs, place, s)]

    far0, far1 = sums([chip(3, 0), chip(3, 1)], flat)
    up_far = along_y(far0, 1)
    down_far = along_y(far1, -1)
    near1, near0 = sums([chip(2, 1), chip(1, 0)], flat)
    up_near = along_y(near1, 1)
    down_near = along_y(near0, -1)
    (last0,) = sums([chip(2, 0) + [up_far]], flat)
    (last1,) = sums([chip(1, 1) + [down_far]], flat)
    up_last = along_y(last0, 1)
    down_last = along_y(last1, -1)
    return sums([chip(0, 0) + [down_near, up_last], chip(0, 1) + [up_near, down_last]], flat, stacked=True)


def solution(mesh):
    tokens = P(None, "seq", "head")
    return jax.shard_map(
        body,
        mesh=mesh,
        in_specs=(tokens,) * 5 + (P(None, "head"),) * 4 + (P("head", None),),
        out_specs=tokens,
        check_vma=False,
    )
```

```python
import jax
import jax.numpy as jnp
from jax import lax
from jax.experimental import pallas as pl
from jax.experimental.pallas import tpu as pltpu
from jax.sharding import PartitionSpec as P

HD = 128
MIB = 1024 * 1024
RELATIVE = (0, -1, 1, 2)


def params(mib=32):
    return pltpu.CompilerParams(vmem_limit_bytes=mib * MIB)


def cost(flops, moved):
    return pl.CostEstimate(flops=int(flops), bytes_accessed=int(moved), transcendentals=0)


def mm(a, b, over_a, over_b):
    return lax.dot_general(
        a, b, (((over_a,), (over_b,)), ((), ())), preferred_element_type=jnp.float32
    )


def nn(a, b):
    return mm(a, b, 1, 0)


def nt(a, b):
    return mm(a, b, 1, 1)


def tn(a, b):
    return mm(a, b, 0, 0)


def whole(shape):
    return pl.BlockSpec(shape, lambda *at: (0,) * len(shape))


def key_state_kernel(k_ref, v_ref, out_ref):
    for s in range(out_ref.shape[0]):
        for h in range(out_ref.shape[1]):
            cols = slice(h * HD, (h + 1) * HD)
            out_ref[s, h] = tn(k_ref[s, :, cols], v_ref[s, :, cols]).astype(out_ref.dtype)


def pick_kernel(table_ref, w_ref, out_ref):
    out_ref[0] = w_ref[...]


def gated_start_kernel(table_ref, g_ref, a0, a1, b0, b1, w_ref, wo_ref, mine_ref, other_ref):
    k = pl.program_id(0)

    @pl.when(k == 0)
    def _():
        for s in range(2):
            mine_ref[s] = nt(g_ref[s], w_ref[...])
            other_ref[s] = nt(g_ref[s], wo_ref[0])

    for at, pair in ((1, (a0, a1)), (2, (b0, b1))):

        @pl.when(k == at)
        def _(pair=pair):
            for s in range(2):
                mine_ref[s] += nt(pair[s][...], w_ref[...])
                other_ref[s] += nt(pair[s][...], wo_ref[0])


def gated_end_kernel(table_ref, mine_in, other_in, c0, c1, w_ref, wo_ref, mine_ref, other_ref):
    for s, piece in enumerate((c0, c1)):
        other_ref[s] = other_in[s] + nt(piece[...], wo_ref[0])
        mine_ref[s] = mine_in[s] + nt(piece[...], w_ref[...])


def gate_kernel(mine_ref, theirs_ref, gate_ref, q_ref, d_out_ref, slope_ref, state_ref):
    for s in range(2):
        d_gated = mine_ref[s] + theirs_ref[s]
        gate_open = jax.nn.sigmoid(gate_ref[s].astype(jnp.float32))
        d_output = d_gated * gate_open
        rounded = d_output.astype(jnp.bfloat16)
        d_out_ref[s] = rounded
        slope_ref[s] = d_output * (1.0 - gate_open)
        for h in range(state_ref.shape[1]):
            cols = slice(h * HD, (h + 1) * HD)
            state_ref[s, h] = tn(q_ref[s, :, cols], rounded[:, cols]).astype(state_ref.dtype)


def make_inner_kernel(factor):
    def inner_kernel(q_ref, k_ref, v_ref, d_out_ref, slope_ref, prefix_ref, dq_ref, dg_ref, dk_ref, dv_ref):
        q, k, v, d_out = q_ref[0], k_ref[0], v_ref[0], d_out_ref[0]
        prefix = prefix_ref[0, 0]
        rows = q.shape[0]
        causal = lax.broadcasted_iota(jnp.int32, (rows, rows), 0) >= lax.broadcasted_iota(
            jnp.int32, (rows, rows), 1
        )
        scores = jnp.where(causal, nt(q, k), 0.0).astype(jnp.bfloat16)
        backward = jnp.where(causal, nt(d_out, v), 0.0).astype(jnp.bfloat16)
        attended = factor * (nn(q, prefix) + nn(scores, v))
        dg_ref[0] = (slope_ref[0] * attended).astype(jnp.bfloat16)
        dq_ref[0] = (factor * (nt(d_out, prefix) + nn(backward, k))).astype(jnp.bfloat16)
        dk_ref[0] = tn(backward, q)
        dv_ref[0] = tn(scores, d_out)

    return inner_kernel


def make_project_kernel(factor):
    def project_kernel(
        table_ref, dq_ref, dg_ref, dk_part, dv_part, k_ref, v_ref, suffix_ref, wq, wk, wv, wg, out_ref, dk_sc, dv_sc
    ):
        seq_count, rows, columns = k_ref.shape

        @pl.when(pl.program_id(0) == 0)
        def _():
            for s in range(seq_count):
                for h in range(columns // HD):
                    cols = slice(h * HD, (h + 1) * HD)
                    suffix = suffix_ref[s, h]
                    dk_sc[s, :, cols] = (
                        factor * (dk_part[s, :, cols] + nt(v_ref[s, :, cols], suffix))
                    ).astype(jnp.bfloat16)
                    dv_sc[s, :, cols] = (
                        factor * (dv_part[s, :, cols] + nn(k_ref[s, :, cols], suffix))
                    ).astype(jnp.bfloat16)

        for s in range(seq_count):
            total = nt(dq_ref[s], wq[...]) + nt(dk_sc[s], wk[...])
            total = total + nt(dv_sc[s], wv[...]) + nt(dg_ref[s], wg[...])
            out_ref[0, s] = total.astype(jnp.bfloat16)

    return project_kernel


def across_seq(state, reverse):
    peers, here = lax.axis_size("seq"), lax.axis_index("seq")

    def swap(x, by):
        return lax.ppermute(x, "seq", [(i, i ^ by) for i in range(peers)])

    def counted(x, bit):
        take = (here & bit) == 0 if reverse else (here & bit) != 0
        return jnp.where(take, x.astype(jnp.float32), 0.0)

    total, entering = state, jnp.zeros(state.shape, jnp.float32)
    for bit, by in ((1, 1), (2, 2), (4, 7)):
        theirs = swap(total, by)
        entering = entering + counted(theirs, bit)
        total = (total.astype(jnp.float32) + theirs.astype(jnp.float32)).astype(jnp.bfloat16)
    swapped = [swap(total, by) for by in (8, 16, 24)]
    for theirs, bit in zip(swapped, (8, 16, 16)):
        entering = entering + counted(theirs, bit)
    return entering.astype(jnp.bfloat16)


def make_sum_kernel(counts):
    def sum_kernel(*refs):
        terms, outs = refs[: sum(counts)], refs[sum(counts) :]
        first = 0
        for at, count in enumerate(counts):
            total = terms[first][...].astype(jnp.float32).reshape(terms[first].shape[-2:])
            for term in terms[first + 1 : first + count]:
                total = total + term[...].astype(jnp.float32).reshape(total.shape)
            if len(outs) == len(counts):
                outs[at][...] = total.astype(jnp.bfloat16)
            else:
                outs[0][at] = total.astype(jnp.bfloat16)
            first += count

    return sum_kernel


def sums(groups, shape, stacked=False):
    arrays, specs = [], []
    for group in groups:
        for term in group:
            if isinstance(term, tuple):
                array, place, s = term
                arrays.append(array)
                specs.append(pl.BlockSpec((1, 1) + shape, lambda i, at=(place, s): at + (0, 0)))
            else:
                arrays.append(term)
                specs.append(whole(shape))
    if stacked:
        outs = jax.ShapeDtypeStruct((len(groups),) + shape, jnp.bfloat16)
        out_specs = whole(outs.shape)
    else:
        outs = [jax.ShapeDtypeStruct(shape, jnp.bfloat16)] * len(groups)
        out_specs = [whole(shape)] * len(groups)
    return pl.pallas_call(
        make_sum_kernel([len(group) for group in groups]),
        out_shape=outs,
        grid=(1,),
        in_specs=specs,
        out_specs=out_specs,
        compiler_params=params(8),
        cost_estimate=cost(0, (len(arrays) + len(groups)) * shape[0] * shape[1] * 2),
    )(*arrays)


def body(queries, keys, values, gate_pre, grad_out, w_query, w_key, w_value, w_gate, w_out):
    seq_count, rows, columns = queries.shape
    head_count = columns // HD
    features = grad_out.shape[2]
    peers = lax.axis_size("head")
    ring = peers // 2
    factor = (lax.axis_size("seq") * rows) ** (-0.5)
    bf16, f32 = jnp.bfloat16, jnp.float32
    state_shape = (seq_count, head_count, HD, HD)
    cube = (seq_count, rows, columns)

    here = lax.axis_index("head")
    y, lane = here // 2, here % 2
    places = jnp.arange(8, dtype=jnp.int32)
    offset = places % 4
    offset = jnp.where(offset == 1, ring - 1, jnp.where(offset == 2, 1, jnp.where(offset == 3, 2, 0)))
    table = 2 * ((y + offset) % ring) + jnp.where(places < 4, 1 - lane, lane)
    table = table.astype(jnp.int32)

    def along_y(x, by):
        return lax.ppermute(x, "head", [(i, (i + 2 * by) % peers) for i in range(peers)])

    def other_core(x):
        return lax.ppermute(x, "head", [(i, i ^ 1) for i in range(peers)])

    g0, g1 = grad_out[0], grad_out[1]
    a0 = along_y(g0, 1)
    b1 = along_y(g1, -1)
    a1 = along_y(g1, 1)
    b0 = along_y(g0, -1)
    c0 = along_y(a0, 1)
    c1 = along_y(b1, -1)

    w_pick = pl.pallas_call(
        pick_kernel,
        out_shape=jax.ShapeDtypeStruct((4, columns, features), bf16),
        grid_spec=pltpu.PrefetchScalarGridSpec(
            num_scalar_prefetch=1,
            grid=(4,),
            in_specs=[pl.BlockSpec((columns, features), lambda k, t: (0, t[k]))],
            out_specs=pl.BlockSpec((1, columns, features), lambda k, t: (k, 0, 0)),
        ),
        compiler_params=params(),
        cost_estimate=cost(0, 2 * 4 * columns * features * 2),
    )(table, w_out)
    w_theirs = other_core(w_pick)

    key_state = pl.pallas_call(
        key_state_kernel,
        out_shape=jax.ShapeDtypeStruct(state_shape, bf16),
        compiler_params=params(),
        cost_estimate=cost(2 * seq_count * rows * columns * HD, 4 * seq_count * rows * columns),
    )(keys, values)
    prefix = across_seq(key_state, False)

    flat = (rows, features)
    two = [jax.ShapeDtypeStruct(cube, f32)] * 2
    piece_flops = 4 * seq_count * rows * features * columns
    mine, other = pl.pallas_call(
        gated_start_kernel,
        out_shape=two,
        grid_spec=pltpu.PrefetchScalarGridSpec(
            num_scalar_prefetch=1,
            grid=(3,),
            in_specs=[whole(grad_out.shape)]
            + [whole(flat)] * 4
            + [
                pl.BlockSpec((columns, features), lambda k, t: (0, t[4 + k])),
                pl.BlockSpec((1, columns, features), lambda k, t: (k, 0, 0)),
            ],
            out_specs=[whole(cube)] * 2,
        ),
        compiler_params=params(),
        cost_estimate=cost(3 * piece_flops, 4 * 1024 * 1024),
    )(table, grad_out, a0, a1, b0, b1, w_out, w_theirs)
    mine, other = pl.pallas_call(
        gated_end_kernel,
        out_shape=two,
        grid_spec=pltpu.PrefetchScalarGridSpec(
            num_scalar_prefetch=1,
            grid=(1,),
            in_specs=[whole(cube)] * 2
            + [whole(flat)] * 2
            + [
                pl.BlockSpec((columns, features), lambda k, t: (0, t[7])),
                pl.BlockSpec((1, columns, features), lambda k, t: (3, 0, 0)),
            ],
            out_specs=[whole(cube)] * 2,
        ),
        compiler_params=params(),
        cost_estimate=cost(piece_flops, 3 * 1024 * 1024),
    )(table, mine, other, c0, c1, w_out, w_theirs)
    theirs = other_core(other)

    d_output, slope, query_state = pl.pallas_call(
        gate_kernel,
        out_shape=[
            jax.ShapeDtypeStruct(cube, bf16),
            jax.ShapeDtypeStruct(cube, f32),
            jax.ShapeDtypeStruct(state_shape, bf16),
        ],
        compiler_params=params(),
        cost_estimate=cost(2 * seq_count * rows * columns * HD, 3 * 1024 * 1024),
    )(mine, theirs, gate_pre, queries)
    suffix = across_seq(query_state, True)

    block = pl.BlockSpec((1, rows, HD), lambda s, h: (s, 0, h))
    d_query, d_gate, dk_part, dv_part = pl.pallas_call(
        make_inner_kernel(factor),
        out_shape=[jax.ShapeDtypeStruct(cube, kind) for kind in (bf16, bf16, f32, f32)],
        grid=(seq_count, head_count),
        in_specs=[block] * 5 + [pl.BlockSpec((1, 1, HD, HD), lambda s, h: (s, h, 0, 0))],
        out_specs=[block] * 4,
        compiler_params=params(),
        cost_estimate=cost(12 * seq_count * rows * rows * columns, 3 * 1024 * 1024),
    )(queries, keys, values, d_output, slope, prefix)

    def project(first):
        weight = pl.BlockSpec((features, columns), lambda k, t: (t[first + k], 0))
        return pl.pallas_call(
            make_project_kernel(factor),
            out_shape=jax.ShapeDtypeStruct((4, seq_count, rows, features), bf16),
            grid_spec=pltpu.PrefetchScalarGridSpec(
                num_scalar_prefetch=1,
                grid=(4,),
                in_specs=[whole(cube)] * 6 + [whole(state_shape)] + [weight] * 4,
                out_specs=pl.BlockSpec((1, seq_count, rows, features), lambda k, t: (k, 0, 0, 0)),
                scratch_shapes=[pltpu.VMEM(cube, bf16)] * 2,
            ),
            compiler_params=params(),
            cost_estimate=cost(32 * seq_count * rows * columns * features, 8 * 1024 * 1024),
        )(table, d_query, d_gate, dk_part, dv_part, keys, values, suffix, w_query, w_key, w_value, w_gate)

    theirs = other_core(project(0))
    own = project(4)

    def chip(place, s):
        return [(own, place, s), (theirs, place, s)]

    far0, far1 = sums([chip(3, 0), chip(3, 1)], flat)
    up_far = along_y(far0, 1)
    down_far = along_y(far1, -1)
    near1, near0 = sums([chip(2, 1), chip(1, 0)], flat)
    up_near = along_y(near1, 1)
    down_near = along_y(near0, -1)
    (last0,) = sums([chip(2, 0) + [up_far]], flat)
    (last1,) = sums([chip(1, 1) + [down_far]], flat)
    up_last = along_y(last0, 1)
    down_last = along_y(last1, -1)
    return sums([chip(0, 0) + [down_near, up_last], chip(0, 1) + [up_near, down_last]], flat, stacked=True)


def solution(mesh):
    tokens = P(None, "seq", "head")
    return jax.shard_map(
        body,
        mesh=mesh,
        in_specs=(tokens,) * 5 + (P(None, "head"),) * 4 + (P("head", None),),
        out_specs=tokens,
        check_vma=False,
    )
```

```python
import jax
import jax.numpy as jnp
from jax import lax
from jax.experimental import pallas as pl
from jax.experimental.pallas import tpu as pltpu
from jax.sharding import PartitionSpec as P

HD = 128
MIB = 1024 * 1024


def params(mib=32):
    return pltpu.CompilerParams(vmem_limit_bytes=mib * MIB)


def cost(flops, moved):
    return pl.CostEstimate(flops=int(flops), bytes_accessed=int(moved), transcendentals=0)


def mm(a, b, over_a, over_b):
    return lax.dot_general(
        a, b, (((over_a,), (over_b,)), ((), ())), preferred_element_type=jnp.float32
    )


def nn(a, b):
    return mm(a, b, 1, 0)


def nt(a, b):
    return mm(a, b, 1, 1)


def tn(a, b):
    return mm(a, b, 0, 0)


def whole(shape):
    return pl.BlockSpec(shape, lambda *at: (0,) * len(shape))


def key_state_kernel(k_ref, v_ref, out_ref):
    for s in range(out_ref.shape[0]):
        for h in range(out_ref.shape[1]):
            cols = slice(h * HD, (h + 1) * HD)
            out_ref[s, h] = tn(k_ref[s, :, cols], v_ref[s, :, cols]).astype(out_ref.dtype)


def pick_kernel(table_ref, w_ref, out_ref):
    out_ref[0] = w_ref[...]


def gated_start_kernel(table_ref, g_ref, a0, a1, b0, b1, w_ref, wo_ref, mine_ref, other_ref):
    k = pl.program_id(0)

    @pl.when(k == 0)
    def _():
        for s in range(2):
            mine_ref[s] = nt(g_ref[s], w_ref[...])
            other_ref[s] = nt(g_ref[s], wo_ref[0])

    for at, pair in ((1, (a0, a1)), (2, (b0, b1))):

        @pl.when(k == at)
        def _(pair=pair):
            for s in range(2):
                mine_ref[s] += nt(pair[s][...], w_ref[...])
                other_ref[s] += nt(pair[s][...], wo_ref[0])


def gated_end_kernel(table_ref, mine_in, other_in, c0, c1, w_ref, wo_ref, mine_ref, other_ref):
    for s, piece in enumerate((c0, c1)):
        other_ref[s] = other_in[s] + nt(piece[...], wo_ref[0])
        mine_ref[s] = mine_in[s] + nt(piece[...], w_ref[...])


def gate_kernel(mine_ref, theirs_ref, gate_ref, q_ref, d_out_ref, slope_ref, state_ref):
    for s in range(2):
        d_gated = mine_ref[s] + theirs_ref[s]
        gate_open = jax.nn.sigmoid(gate_ref[s].astype(jnp.float32))
        d_output = d_gated * gate_open
        rounded = d_output.astype(jnp.bfloat16)
        d_out_ref[s] = rounded
        slope_ref[s] = d_output * (1.0 - gate_open)
        for h in range(state_ref.shape[1]):
            cols = slice(h * HD, (h + 1) * HD)
            state_ref[s, h] = tn(q_ref[s, :, cols], rounded[:, cols]).astype(state_ref.dtype)


def make_inner_kernel(factor):
    def inner_kernel(q_ref, k_ref, v_ref, d_out_ref, slope_ref, prefix_ref, dq_ref, dg_ref, dk_ref, dv_ref):
        q, k, v, d_out = q_ref[0], k_ref[0], v_ref[0], d_out_ref[0]
        prefix = prefix_ref[0, 0]
        rows = q.shape[0]
        causal = lax.broadcasted_iota(jnp.int32, (rows, rows), 0) >= lax.broadcasted_iota(
            jnp.int32, (rows, rows), 1
        )
        scores = jnp.where(causal, nt(q, k), 0.0).astype(jnp.bfloat16)
        backward = jnp.where(causal, nt(d_out, v), 0.0).astype(jnp.bfloat16)
        attended = factor * (nn(q, prefix) + nn(scores, v))
        dg_ref[0] = (slope_ref[0] * attended).astype(jnp.bfloat16)
        dq_ref[0] = (factor * (nt(d_out, prefix) + nn(backward, k))).astype(jnp.bfloat16)
        dk_ref[0] = tn(backward, q)
        dv_ref[0] = tn(scores, d_out)

    return inner_kernel


def make_project_kernel(factor):
    def project_kernel(
        table_ref, dq_ref, dg_ref, dk_part, dv_part, k_ref, v_ref, suffix_ref, wq, wk, wv, wg, out_ref, dk_sc, dv_sc
    ):
        seq_count, rows, columns = k_ref.shape

        @pl.when(pl.program_id(0) == 0)
        def _():
            for s in range(seq_count):
                for h in range(columns // HD):
                    cols = slice(h * HD, (h + 1) * HD)
                    suffix = suffix_ref[s, h]
                    dk_sc[s, :, cols] = (
                        factor * (dk_part[s, :, cols] + nt(v_ref[s, :, cols], suffix))
                    ).astype(jnp.bfloat16)
                    dv_sc[s, :, cols] = (
                        factor * (dv_part[s, :, cols] + nn(k_ref[s, :, cols], suffix))
                    ).astype(jnp.bfloat16)

        for s in range(seq_count):
            total = nt(dq_ref[s], wq[...]) + nt(dk_sc[s], wk[...])
            total = total + nt(dv_sc[s], wv[...]) + nt(dg_ref[s], wg[...])
            out_ref[0, s] = total.astype(jnp.bfloat16)

    return project_kernel


def across_seq(state, reverse):
    peers, here = lax.axis_size("seq"), lax.axis_index("seq")

    def swap(x, by):
        return lax.ppermute(x, "seq", [(i, i ^ by) for i in range(peers)])

    def counted(x, bit):
        take = (here & bit) == 0 if reverse else (here & bit) != 0
        return jnp.where(take, x.astype(jnp.float32), 0.0)

    total, entering = state, jnp.zeros(state.shape, jnp.float32)
    for bit in (1, 2, 4):
        theirs = swap(total, bit)
        entering = entering + counted(theirs, bit)
        total = (total.astype(jnp.float32) + theirs.astype(jnp.float32)).astype(jnp.bfloat16)
    swapped = [swap(total, by) for by in (8, 16, 24)]
    for theirs, bit in zip(swapped, (8, 16, 16)):
        entering = entering + counted(theirs, bit)
    return entering.astype(jnp.bfloat16)


def make_sum_kernel(counts):
    def sum_kernel(*refs):
        terms, outs = refs[: sum(counts)], refs[sum(counts) :]
        first = 0
        for at, count in enumerate(counts):
            total = terms[first][...].astype(jnp.float32).reshape(terms[first].shape[-2:])
            for term in terms[first + 1 : first + count]:
                total = total + term[...].astype(jnp.float32).reshape(total.shape)
            if len(outs) == len(counts):
                outs[at][...] = total.astype(jnp.bfloat16)
            else:
                outs[0][at] = total.astype(jnp.bfloat16)
            first += count

    return sum_kernel


def sums(groups, shape, stacked=False):
    arrays, specs = [], []
    for group in groups:
        for term in group:
            if isinstance(term, tuple):
                array, place, s = term
                arrays.append(array)
                specs.append(pl.BlockSpec((1, 1) + shape, lambda i, at=(place, s): at + (0, 0)))
            else:
                arrays.append(term)
                specs.append(whole(shape))
    if stacked:
        outs = jax.ShapeDtypeStruct((len(groups),) + shape, jnp.bfloat16)
        out_specs = whole(outs.shape)
    else:
        outs = [jax.ShapeDtypeStruct(shape, jnp.bfloat16)] * len(groups)
        out_specs = [whole(shape)] * len(groups)
    return pl.pallas_call(
        make_sum_kernel([len(group) for group in groups]),
        out_shape=outs,
        grid=(1,),
        in_specs=specs,
        out_specs=out_specs,
        compiler_params=params(8),
        cost_estimate=cost(0, (len(arrays) + len(groups)) * shape[0] * shape[1] * 2),
    )(*arrays)


def body(queries, keys, values, gate_pre, grad_out, w_query, w_key, w_value, w_gate, w_out):
    seq_count, rows, columns = queries.shape
    head_count = columns // HD
    features = grad_out.shape[2]
    peers = lax.axis_size("head")
    factor = (lax.axis_size("seq") * rows) ** (-0.5)
    bf16, f32 = jnp.bfloat16, jnp.float32
    state_shape = (seq_count, head_count, HD, HD)
    cube = (seq_count, rows, columns)

    here = lax.axis_index("head")
    y, lane = here // 2, here % 2
    places = jnp.arange(8, dtype=jnp.int32)
    offset = places % 4
    offset = offset ^ (offset >> 1)
    table = 2 * (y ^ offset) + jnp.where(places < 4, 1 - lane, lane)
    table = table.astype(jnp.int32)

    def along_y(x, by):
        return lax.ppermute(x, "head", [(i, i ^ (2 * by)) for i in range(peers)])

    def other_core(x):
        return lax.ppermute(x, "head", [(i, i ^ 1) for i in range(peers)])

    g0, g1 = grad_out[0], grad_out[1]
    a0 = along_y(g0, 1)
    b1 = along_y(g1, 3)
    a1 = along_y(g1, 1)
    b0 = along_y(g0, 3)
    c0 = along_y(a0, 3)
    c1 = along_y(b1, 1)

    w_pick = pl.pallas_call(
        pick_kernel,
        out_shape=jax.ShapeDtypeStruct((4, columns, features), bf16),
        grid_spec=pltpu.PrefetchScalarGridSpec(
            num_scalar_prefetch=1,
            grid=(4,),
            in_specs=[pl.BlockSpec((columns, features), lambda k, t: (0, t[k]))],
            out_specs=pl.BlockSpec((1, columns, features), lambda k, t: (k, 0, 0)),
        ),
        compiler_params=params(),
        cost_estimate=cost(0, 2 * 4 * columns * features * 2),
    )(table, w_out)
    w_theirs = other_core(w_pick)

    key_state = pl.pallas_call(
        key_state_kernel,
        out_shape=jax.ShapeDtypeStruct(state_shape, bf16),
        compiler_params=params(),
        cost_estimate=cost(2 * seq_count * rows * columns * HD, 4 * seq_count * rows * columns),
    )(keys, values)
    prefix = across_seq(key_state, False)

    flat = (rows, features)
    two = [jax.ShapeDtypeStruct(cube, f32)] * 2
    piece_flops = 4 * seq_count * rows * features * columns
    mine, other = pl.pallas_call(
        gated_start_kernel,
        out_shape=two,
        grid_spec=pltpu.PrefetchScalarGridSpec(
            num_scalar_prefetch=1,
            grid=(3,),
            in_specs=[whole(grad_out.shape)]
            + [whole(flat)] * 4
            + [
                pl.BlockSpec((columns, features), lambda k, t: (0, t[4 + k])),
                pl.BlockSpec((1, columns, features), lambda k, t: (k, 0, 0)),
            ],
            out_specs=[whole(cube)] * 2,
        ),
        compiler_params=params(),
        cost_estimate=cost(3 * piece_flops, 4 * 1024 * 1024),
    )(table, grad_out, a0, a1, b0, b1, w_out, w_theirs)
    mine, other = pl.pallas_call(
        gated_end_kernel,
        out_shape=two,
        grid_spec=pltpu.PrefetchScalarGridSpec(
            num_scalar_prefetch=1,
            grid=(1,),
            in_specs=[whole(cube)] * 2
            + [whole(flat)] * 2
            + [
                pl.BlockSpec((columns, features), lambda k, t: (0, t[7])),
                pl.BlockSpec((1, columns, features), lambda k, t: (3, 0, 0)),
            ],
            out_specs=[whole(cube)] * 2,
        ),
        compiler_params=params(),
        cost_estimate=cost(piece_flops, 3 * 1024 * 1024),
    )(table, mine, other, c0, c1, w_out, w_theirs)
    theirs = other_core(other)

    d_output, slope, query_state = pl.pallas_call(
        gate_kernel,
        out_shape=[
            jax.ShapeDtypeStruct(cube, bf16),
            jax.ShapeDtypeStruct(cube, f32),
            jax.ShapeDtypeStruct(state_shape, bf16),
        ],
        compiler_params=params(),
        cost_estimate=cost(2 * seq_count * rows * columns * HD, 3 * 1024 * 1024),
    )(mine, theirs, gate_pre, queries)
    suffix = across_seq(query_state, True)

    block = pl.BlockSpec((1, rows, HD), lambda s, h: (s, 0, h))
    d_query, d_gate, dk_part, dv_part = pl.pallas_call(
        make_inner_kernel(factor),
        out_shape=[jax.ShapeDtypeStruct(cube, kind) for kind in (bf16, bf16, f32, f32)],
        grid=(seq_count, head_count),
        in_specs=[block] * 5 + [pl.BlockSpec((1, 1, HD, HD), lambda s, h: (s, h, 0, 0))],
        out_specs=[block] * 4,
        compiler_params=params(),
        cost_estimate=cost(12 * seq_count * rows * rows * columns, 3 * 1024 * 1024),
    )(queries, keys, values, d_output, slope, prefix)

    def project(first):
        weight = pl.BlockSpec((features, columns), lambda k, t: (t[first + k], 0))
        return pl.pallas_call(
            make_project_kernel(factor),
            out_shape=jax.ShapeDtypeStruct((4, seq_count, rows, features), bf16),
            grid_spec=pltpu.PrefetchScalarGridSpec(
                num_scalar_prefetch=1,
                grid=(4,),
                in_specs=[whole(cube)] * 6 + [whole(state_shape)] + [weight] * 4,
                out_specs=pl.BlockSpec((1, seq_count, rows, features), lambda k, t: (k, 0, 0, 0)),
                scratch_shapes=[pltpu.VMEM(cube, bf16)] * 2,
            ),
            compiler_params=params(),
            cost_estimate=cost(32 * seq_count * rows * columns * features, 8 * 1024 * 1024),
        )(table, d_query, d_gate, dk_part, dv_part, keys, values, suffix, w_query, w_key, w_value, w_gate)

    theirs = other_core(project(0))
    own = project(4)

    def chip(place, s):
        return [(own, place, s), (theirs, place, s)]

    far0, far1 = sums([chip(3, 0), chip(3, 1)], flat)
    through0 = along_y(far0, 1)
    through1 = along_y(far1, 3)
    near0, near1 = sums([chip(1, 0), chip(2, 1)], flat)
    direct0 = along_y(near0, 1)
    direct1 = along_y(near1, 3)
    (last0,) = sums([chip(2, 0) + [through0]], flat)
    (last1,) = sums([chip(1, 1) + [through1]], flat)
    joined0 = along_y(last0, 3)
    joined1 = along_y(last1, 1)
    return sums([chip(0, 0) + [direct0, joined0], chip(0, 1) + [direct1, joined1]], flat, stacked=True)


def solution(mesh):
    tokens = P(None, "seq", "head")
    return jax.shard_map(
        body,
        mesh=mesh,
        in_specs=(tokens,) * 5 + (P(None, "head"),) * 4 + (P("head", None),),
        out_specs=tokens,
        check_vma=False,
    )
```

```python
import jax
import jax.numpy as jnp
from jax import lax
from jax.experimental import pallas as pl
from jax.experimental.pallas import tpu as pltpu
from jax.sharding import PartitionSpec as P

HD = 128
MIB = 1024 * 1024


def params(mib=8):
    return pltpu.CompilerParams(vmem_limit_bytes=mib * MIB)


def cost(flops, moved):
    return pl.CostEstimate(flops=int(flops), bytes_accessed=int(moved), transcendentals=0)


def mm(a, b, over_a, over_b):
    return lax.dot_general(
        a, b, (((over_a,), (over_b,)), ((), ())), preferred_element_type=jnp.float32
    )


def nn(a, b):
    return mm(a, b, 1, 0)


def nt(a, b):
    return mm(a, b, 1, 1)


def tn(a, b):
    return mm(a, b, 0, 0)


def whole(shape):
    return pl.BlockSpec(shape, lambda *at: (0,) * len(shape))


def key_state_kernel(k_ref, v_ref, out_ref):
    for s in range(out_ref.shape[0]):
        for h in range(out_ref.shape[1]):
            cols = slice(h * HD, (h + 1) * HD)
            out_ref[s, h] = tn(k_ref[s, :, cols], v_ref[s, :, cols]).astype(out_ref.dtype)


def pick_kernel(table_ref, w_ref, out_ref):
    out_ref[0] = w_ref[...]


def gated_start_kernel(table_ref, g_ref, a0, a1, b0, b1, w_ref, wo_ref, mine_ref, other_ref):
    k = pl.program_id(0)

    @pl.when(k == 0)
    def _():
        for s in range(2):
            mine_ref[s] = nt(g_ref[s], w_ref[...])
            other_ref[s] = nt(g_ref[s], wo_ref[0])

    for at, pair in ((1, (a0, a1)), (2, (b0, b1))):

        @pl.when(k == at)
        def _(pair=pair):
            for s in range(2):
                mine_ref[s] += nt(pair[s][...], w_ref[...])
                other_ref[s] += nt(pair[s][...], wo_ref[0])


def gated_end_kernel(table_ref, mine_in, other_in, c0, c1, w_ref, wo_ref, mine_ref, other_ref):
    for s, piece in enumerate((c0, c1)):
        other_ref[s] = other_in[s] + nt(piece[...], wo_ref[0])
        mine_ref[s] = mine_in[s] + nt(piece[...], w_ref[...])


def gate_kernel(mine_ref, theirs_ref, gate_ref, q_ref, d_out_ref, slope_ref, state_ref):
    for s in range(2):
        d_gated = mine_ref[s] + theirs_ref[s]
        gate_open = jax.nn.sigmoid(gate_ref[s].astype(jnp.float32))
        d_output = d_gated * gate_open
        rounded = d_output.astype(jnp.bfloat16)
        d_out_ref[s] = rounded
        slope_ref[s] = d_output * (1.0 - gate_open)
        for h in range(state_ref.shape[1]):
            cols = slice(h * HD, (h + 1) * HD)
            state_ref[s, h] = tn(q_ref[s, :, cols], rounded[:, cols]).astype(state_ref.dtype)


def make_inner_kernel(factor):
    def inner_kernel(q_ref, k_ref, v_ref, d_out_ref, slope_ref, prefix_ref, dq_ref, dg_ref, dk_ref, dv_ref):
        q, k, v, d_out = q_ref[0], k_ref[0], v_ref[0], d_out_ref[0]
        prefix = prefix_ref[0, 0]
        rows = q.shape[0]
        causal = lax.broadcasted_iota(jnp.int32, (rows, rows), 0) >= lax.broadcasted_iota(
            jnp.int32, (rows, rows), 1
        )
        scores = jnp.where(causal, nt(q, k), 0.0).astype(jnp.bfloat16)
        backward = jnp.where(causal, nt(d_out, v), 0.0).astype(jnp.bfloat16)
        attended = factor * (nn(q, prefix) + nn(scores, v))
        dg_ref[0] = (slope_ref[0] * attended).astype(jnp.bfloat16)
        dq_ref[0] = (factor * (nt(d_out, prefix) + nn(backward, k))).astype(jnp.bfloat16)
        dk_ref[0] = tn(backward, q)
        dv_ref[0] = tn(scores, d_out)

    return inner_kernel


def make_project_kernel(factor):
    def project_kernel(
        table_ref, dq_ref, dg_ref, dk_part, dv_part, k_ref, v_ref, suffix_ref, wq, wk, wv, wg, out_ref, dk_sc, dv_sc
    ):
        seq_count, rows, columns = k_ref.shape

        @pl.when(pl.program_id(0) == 0)
        def _():
            for s in range(seq_count):
                for h in range(columns // HD):
                    cols = slice(h * HD, (h + 1) * HD)
                    suffix = suffix_ref[s, h]
                    dk_sc[s, :, cols] = (
                        factor * (dk_part[s, :, cols] + nt(v_ref[s, :, cols], suffix))
                    ).astype(jnp.bfloat16)
                    dv_sc[s, :, cols] = (
                        factor * (dv_part[s, :, cols] + nn(k_ref[s, :, cols], suffix))
                    ).astype(jnp.bfloat16)

        for s in range(seq_count):
            total = nt(dq_ref[s], wq[...]) + nt(dk_sc[s], wk[...])
            total = total + nt(dv_sc[s], wv[...]) + nt(dg_ref[s], wg[...])
            out_ref[0, s] = total.astype(jnp.bfloat16)

    return project_kernel


def across_seq(state, reverse):
    peers, here = lax.axis_size("seq"), lax.axis_index("seq")

    def swap(x, by):
        return lax.ppermute(x, "seq", [(i, i ^ by) for i in range(peers)])

    def counted(x, bit):
        take = (here & bit) == 0 if reverse else (here & bit) != 0
        return jnp.where(take, x.astype(jnp.float32), 0.0)

    odd = (here & 1) != 0
    kept = jnp.where(odd, state[:, 1], state[:, 0])
    theirs = swap(jnp.where(odd, state[:, 0], state[:, 1]), 1)
    total = (kept.astype(jnp.float32) + theirs.astype(jnp.float32)).astype(jnp.bfloat16)
    entering = jnp.zeros(kept.shape, jnp.float32)
    for bit in (2, 4):
        peer = swap(total, bit)
        entering = entering + counted(peer, bit)
        total = (total.astype(jnp.float32) + peer.astype(jnp.float32)).astype(jnp.bfloat16)
    swapped = [swap(total, by) for by in (8, 16, 24)]
    for peer, bit in zip(swapped, (8, 16, 16)):
        entering = entering + counted(peer, bit)
    meets = jnp.logical_not(odd) if reverse else odd
    mine = (entering + jnp.where(meets, theirs.astype(jnp.float32), 0.0)).astype(jnp.bfloat16)
    partners = (entering + jnp.where(meets, 0.0, kept.astype(jnp.float32))).astype(jnp.bfloat16)
    other = swap(partners, 1)
    return jnp.stack([jnp.where(odd, other, mine), jnp.where(odd, mine, other)], axis=1)


def make_sum_kernel(counts):
    def sum_kernel(*refs):
        terms, outs = refs[: sum(counts)], refs[sum(counts) :]
        first = 0
        for at, count in enumerate(counts):
            total = terms[first][...].astype(jnp.float32).reshape(terms[first].shape[-2:])
            for term in terms[first + 1 : first + count]:
                total = total + term[...].astype(jnp.float32).reshape(total.shape)
            if len(outs) == len(counts):
                outs[at][...] = total.astype(jnp.bfloat16)
            else:
                outs[0][at] = total.astype(jnp.bfloat16)
            first += count

    return sum_kernel


def sums(groups, shape, stacked=False):
    arrays, specs = [], []
    for group in groups:
        for term in group:
            if isinstance(term, tuple):
                array, place, s = term
                arrays.append(array)
                specs.append(pl.BlockSpec((1, 1) + shape, lambda i, at=(place, s): at + (0, 0)))
            else:
                arrays.append(term)
                specs.append(whole(shape))
    if stacked:
        outs = jax.ShapeDtypeStruct((len(groups),) + shape, jnp.bfloat16)
        out_specs = whole(outs.shape)
    else:
        outs = [jax.ShapeDtypeStruct(shape, jnp.bfloat16)] * len(groups)
        out_specs = [whole(shape)] * len(groups)
    return pl.pallas_call(
        make_sum_kernel([len(group) for group in groups]),
        out_shape=outs,
        grid=(1,),
        in_specs=specs,
        out_specs=out_specs,
        compiler_params=params(8),
        cost_estimate=cost(0, (len(arrays) + len(groups)) * shape[0] * shape[1] * 2),
    )(*arrays)


def body(queries, keys, values, gate_pre, grad_out, w_query, w_key, w_value, w_gate, w_out):
    seq_count, rows, columns = queries.shape
    head_count = columns // HD
    features = grad_out.shape[2]
    peers = lax.axis_size("head")
    factor = (lax.axis_size("seq") * rows) ** (-0.5)
    bf16, f32 = jnp.bfloat16, jnp.float32
    state_shape = (seq_count, head_count, HD, HD)
    cube = (seq_count, rows, columns)

    here = lax.axis_index("head")
    y, lane = here // 2, here % 2
    places = jnp.arange(8, dtype=jnp.int32)
    offset = places % 4
    offset = offset ^ (offset >> 1)
    table = 2 * (y ^ offset) + jnp.where(places < 4, 1 - lane, lane)
    table = table.astype(jnp.int32)

    def along_y(x, by):
        return lax.ppermute(x, "head", [(i, i ^ (2 * by)) for i in range(peers)])

    def other_core(x):
        return lax.ppermute(x, "head", [(i, i ^ 1) for i in range(peers)])

    g0, g1 = grad_out[0], grad_out[1]
    a0 = along_y(g0, 1)
    b1 = along_y(g1, 3)
    a1 = along_y(g1, 1)
    b0 = along_y(g0, 3)
    c0 = along_y(a0, 3)
    c1 = along_y(b1, 1)

    w_pick = pl.pallas_call(
        pick_kernel,
        out_shape=jax.ShapeDtypeStruct((4, columns, features), bf16),
        grid_spec=pltpu.PrefetchScalarGridSpec(
            num_scalar_prefetch=1,
            grid=(4,),
            in_specs=[pl.BlockSpec((columns, features), lambda k, t: (0, t[k]))],
            out_specs=pl.BlockSpec((1, columns, features), lambda k, t: (k, 0, 0)),
        ),
        compiler_params=params(),
        cost_estimate=cost(0, 2 * 4 * columns * features * 2),
    )(table, w_out)
    w_theirs = other_core(w_pick)

    key_state = pl.pallas_call(
        key_state_kernel,
        out_shape=jax.ShapeDtypeStruct(state_shape, bf16),
        compiler_params=params(),
        cost_estimate=cost(2 * seq_count * rows * columns * HD, 4 * seq_count * rows * columns),
    )(keys, values)
    prefix = across_seq(key_state, False)

    flat = (rows, features)
    two = [jax.ShapeDtypeStruct(cube, f32)] * 2
    piece_flops = 4 * seq_count * rows * features * columns
    mine, other = pl.pallas_call(
        gated_start_kernel,
        out_shape=two,
        grid_spec=pltpu.PrefetchScalarGridSpec(
            num_scalar_prefetch=1,
            grid=(3,),
            in_specs=[whole(grad_out.shape)]
            + [whole(flat)] * 4
            + [
                pl.BlockSpec((columns, features), lambda k, t: (0, t[4 + k])),
                pl.BlockSpec((1, columns, features), lambda k, t: (k, 0, 0)),
            ],
            out_specs=[whole(cube)] * 2,
        ),
        compiler_params=params(),
        cost_estimate=cost(3 * piece_flops, 4 * 1024 * 1024),
    )(table, grad_out, a0, a1, b0, b1, w_out, w_theirs)
    mine, other = pl.pallas_call(
        gated_end_kernel,
        out_shape=two,
        grid_spec=pltpu.PrefetchScalarGridSpec(
            num_scalar_prefetch=1,
            grid=(1,),
            in_specs=[whole(cube)] * 2
            + [whole(flat)] * 2
            + [
                pl.BlockSpec((columns, features), lambda k, t: (0, t[7])),
                pl.BlockSpec((1, columns, features), lambda k, t: (3, 0, 0)),
            ],
            out_specs=[whole(cube)] * 2,
        ),
        compiler_params=params(),
        cost_estimate=cost(piece_flops, 3 * 1024 * 1024),
    )(table, mine, other, c0, c1, w_out, w_theirs)
    theirs = other_core(other)

    d_output, slope, query_state = pl.pallas_call(
        gate_kernel,
        out_shape=[
            jax.ShapeDtypeStruct(cube, bf16),
            jax.ShapeDtypeStruct(cube, f32),
            jax.ShapeDtypeStruct(state_shape, bf16),
        ],
        compiler_params=params(),
        cost_estimate=cost(2 * seq_count * rows * columns * HD, 3 * 1024 * 1024),
    )(mine, theirs, gate_pre, queries)
    suffix = across_seq(query_state, True)

    block = pl.BlockSpec((1, rows, HD), lambda s, h: (s, 0, h))
    d_query, d_gate, dk_part, dv_part = pl.pallas_call(
        make_inner_kernel(factor),
        out_shape=[jax.ShapeDtypeStruct(cube, kind) for kind in (bf16, bf16, f32, f32)],
        grid=(seq_count, head_count),
        in_specs=[block] * 5 + [pl.BlockSpec((1, 1, HD, HD), lambda s, h: (s, h, 0, 0))],
        out_specs=[block] * 4,
        compiler_params=params(48),
        cost_estimate=cost(12 * seq_count * rows * rows * columns, 3 * 1024 * 1024),
    )(queries, keys, values, d_output, slope, prefix)

    def project(first):
        weight = pl.BlockSpec((features, columns), lambda k, t: (t[first + k], 0))
        return pl.pallas_call(
            make_project_kernel(factor),
            out_shape=jax.ShapeDtypeStruct((4, seq_count, rows, features), bf16),
            grid_spec=pltpu.PrefetchScalarGridSpec(
                num_scalar_prefetch=1,
                grid=(4,),
                in_specs=[whole(cube)] * 6 + [whole(state_shape)] + [weight] * 4,
                out_specs=pl.BlockSpec((1, seq_count, rows, features), lambda k, t: (k, 0, 0, 0)),
                scratch_shapes=[pltpu.VMEM(cube, bf16)] * 2,
            ),
            compiler_params=params(48),
            cost_estimate=cost(32 * seq_count * rows * columns * features, 8 * 1024 * 1024),
        )(table, d_query, d_gate, dk_part, dv_part, keys, values, suffix, w_query, w_key, w_value, w_gate)

    theirs = other_core(project(0))
    own = project(4)

    def chip(place, s):
        return [(own, place, s), (theirs, place, s)]

    far0, far1 = sums([chip(3, 0), chip(3, 1)], flat)
    through0 = along_y(far0, 1)
    through1 = along_y(far1, 3)
    near0, near1 = sums([chip(1, 0), chip(2, 1)], flat)
    direct0 = along_y(near0, 1)
    direct1 = along_y(near1, 3)
    (last0,) = sums([chip(2, 0) + [through0]], flat)
    (last1,) = sums([chip(1, 1) + [through1]], flat)
    joined0 = along_y(last0, 3)
    joined1 = along_y(last1, 1)
    return sums([chip(0, 0) + [direct0, joined0], chip(0, 1) + [direct1, joined1]], flat, stacked=True)


def solution(mesh):
    tokens = P(None, "seq", "head")
    return jax.shard_map(
        body,
        mesh=mesh,
        in_specs=(tokens,) * 5 + (P(None, "head"),) * 4 + (P("head", None),),
        out_specs=tokens,
        check_vma=False,
    )
```

```python
import jax
import jax.numpy as jnp
from jax import lax
from jax.experimental import pallas as pl
from jax.experimental.pallas import tpu as pltpu
from jax.sharding import PartitionSpec as P

HD = 128
MIB = 1024 * 1024


def params(mib=32):
    return pltpu.CompilerParams(vmem_limit_bytes=mib * MIB)


def cost(flops, moved):
    return pl.CostEstimate(flops=int(flops), bytes_accessed=int(moved), transcendentals=0)


def mm(a, b, over_a, over_b):
    return lax.dot_general(
        a, b, (((over_a,), (over_b,)), ((), ())), preferred_element_type=jnp.float32
    )


def nn(a, b):
    return mm(a, b, 1, 0)


def nt(a, b):
    return mm(a, b, 1, 1)


def tn(a, b):
    return mm(a, b, 0, 0)


def whole(shape):
    return pl.BlockSpec(shape, lambda *at: (0,) * len(shape))


def key_state_kernel(k_ref, v_ref, out_ref):
    for s in range(out_ref.shape[0]):
        for h in range(out_ref.shape[1]):
            cols = slice(h * HD, (h + 1) * HD)
            out_ref[s, h] = tn(k_ref[s, :, cols], v_ref[s, :, cols]).astype(out_ref.dtype)


def pick_kernel(table_ref, w_ref, out_ref):
    out_ref[0] = w_ref[...]


def gated_start_kernel(table_ref, g_ref, a0, a1, b0, b1, w_ref, wo_ref, mine_ref, other_ref):
    k = pl.program_id(0)

    @pl.when(k == 0)
    def _():
        for s in range(2):
            mine_ref[s] = nt(g_ref[s], w_ref[...])
            other_ref[s] = nt(g_ref[s], wo_ref[0])

    for at, pair in ((1, (a0, a1)), (2, (b0, b1))):

        @pl.when(k == at)
        def _(pair=pair):
            for s in range(2):
                mine_ref[s] += nt(pair[s][...], w_ref[...])
                other_ref[s] += nt(pair[s][...], wo_ref[0])


def gated_end_kernel(table_ref, mine_in, other_in, c0, c1, w_ref, wo_ref, mine_ref, other_ref):
    for s, piece in enumerate((c0, c1)):
        other_ref[s] = other_in[s] + nt(piece[...], wo_ref[0])
        mine_ref[s] = mine_in[s] + nt(piece[...], w_ref[...])


def gate_kernel(mine_ref, theirs_ref, gate_ref, q_ref, d_out_ref, slope_ref, state_ref):
    for s in range(2):
        d_gated = mine_ref[s] + theirs_ref[s]
        gate_open = jax.nn.sigmoid(gate_ref[s].astype(jnp.float32))
        d_output = d_gated * gate_open
        rounded = d_output.astype(jnp.bfloat16)
        d_out_ref[s] = rounded
        slope_ref[s] = d_output * (1.0 - gate_open)
        for h in range(state_ref.shape[1]):
            cols = slice(h * HD, (h + 1) * HD)
            state_ref[s, h] = tn(q_ref[s, :, cols], rounded[:, cols]).astype(state_ref.dtype)


def make_inner_kernel(factor):
    def inner_kernel(q_ref, k_ref, v_ref, d_out_ref, slope_ref, prefix_ref, dq_ref, dg_ref, dk_ref, dv_ref):
        q, k, v, d_out = q_ref[0], k_ref[0], v_ref[0], d_out_ref[0]
        prefix = prefix_ref[0, 0]
        rows = q.shape[0]
        causal = lax.broadcasted_iota(jnp.int32, (rows, rows), 0) >= lax.broadcasted_iota(
            jnp.int32, (rows, rows), 1
        )
        scores = jnp.where(causal, nt(q, k), 0.0).astype(jnp.bfloat16)
        backward = jnp.where(causal, nt(d_out, v), 0.0).astype(jnp.bfloat16)
        attended = factor * (nn(q, prefix) + nn(scores, v))
        dg_ref[0] = (slope_ref[0] * attended).astype(jnp.bfloat16)
        dq_ref[0] = (factor * (nt(d_out, prefix) + nn(backward, k))).astype(jnp.bfloat16)
        dk_ref[0] = tn(backward, q)
        dv_ref[0] = tn(scores, d_out)

    return inner_kernel


def make_project_kernel(factor):
    def project_kernel(
        table_ref, dq_ref, dg_ref, dk_part, dv_part, k_ref, v_ref, suffix_ref, wq, wk, wv, wg, out_ref, dk_sc, dv_sc
    ):
        seq_count, rows, columns = k_ref.shape

        @pl.when(pl.program_id(0) == 0)
        def _():
            for s in range(seq_count):
                for h in range(columns // HD):
                    cols = slice(h * HD, (h + 1) * HD)
                    suffix = suffix_ref[s, h]
                    dk_sc[s, :, cols] = (
                        factor * (dk_part[s, :, cols] + nt(v_ref[s, :, cols], suffix))
                    ).astype(jnp.bfloat16)
                    dv_sc[s, :, cols] = (
                        factor * (dv_part[s, :, cols] + nn(k_ref[s, :, cols], suffix))
                    ).astype(jnp.bfloat16)

        for s in range(seq_count):
            total = nt(dq_ref[s], wq[...]) + nt(dk_sc[s], wk[...])
            total = total + nt(dv_sc[s], wv[...]) + nt(dg_ref[s], wg[...])
            out_ref[0, s] = total.astype(jnp.bfloat16)

    return project_kernel


def across_seq(state, reverse, behind=None):
    peers, here = lax.axis_size("seq"), lax.axis_index("seq")

    def swap(x, by):
        return lax.ppermute(x, "seq", [(i, i ^ by) for i in range(peers)])

    def counted(x, bit):
        take = (here & bit) == 0 if reverse else (here & bit) != 0
        return jnp.where(take, x.astype(jnp.float32), 0.0)

    odd = (here & 1) != 0
    kept = jnp.where(odd, state[:, 1], state[:, 0])
    theirs = swap(jnp.where(odd, state[:, 0], state[:, 1]), 1)
    if behind is not None:
        theirs, _ = lax.optimization_barrier((theirs, behind))
    total = (kept.astype(jnp.float32) + theirs.astype(jnp.float32)).astype(jnp.bfloat16)
    entering = jnp.zeros(kept.shape, jnp.float32)
    for bit in (2, 4):
        peer = swap(total, bit)
        entering = entering + counted(peer, bit)
        total = (total.astype(jnp.float32) + peer.astype(jnp.float32)).astype(jnp.bfloat16)
    swapped = [swap(total, by) for by in (8, 16, 24)]
    for peer, bit in zip(swapped, (8, 16, 16)):
        entering = entering + counted(peer, bit)
    meets = jnp.logical_not(odd) if reverse else odd
    mine = (entering + jnp.where(meets, theirs.astype(jnp.float32), 0.0)).astype(jnp.bfloat16)
    partners = (entering + jnp.where(meets, 0.0, kept.astype(jnp.float32))).astype(jnp.bfloat16)
    other = swap(partners, 1)
    return jnp.stack([jnp.where(odd, other, mine), jnp.where(odd, mine, other)], axis=1)


def make_sum_kernel(counts):
    def sum_kernel(*refs):
        terms, outs = refs[: sum(counts)], refs[sum(counts) :]
        first = 0
        for at, count in enumerate(counts):
            total = terms[first][...].astype(jnp.float32).reshape(terms[first].shape[-2:])
            for term in terms[first + 1 : first + count]:
                total = total + term[...].astype(jnp.float32).reshape(total.shape)
            if len(outs) == len(counts):
                outs[at][...] = total.astype(jnp.bfloat16)
            else:
                outs[0][at] = total.astype(jnp.bfloat16)
            first += count

    return sum_kernel


def sums(groups, shape, stacked=False):
    arrays, specs = [], []
    for group in groups:
        for term in group:
            if isinstance(term, tuple):
                array, place, s = term
                arrays.append(array)
                specs.append(pl.BlockSpec((1, 1) + shape, lambda i, at=(place, s): at + (0, 0)))
            else:
                arrays.append(term)
                specs.append(whole(shape))
    if stacked:
        outs = jax.ShapeDtypeStruct((len(groups),) + shape, jnp.bfloat16)
        out_specs = whole(outs.shape)
    else:
        outs = [jax.ShapeDtypeStruct(shape, jnp.bfloat16)] * len(groups)
        out_specs = [whole(shape)] * len(groups)
    return pl.pallas_call(
        make_sum_kernel([len(group) for group in groups]),
        out_shape=outs,
        grid=(1,),
        in_specs=specs,
        out_specs=out_specs,
        compiler_params=params(8),
        cost_estimate=cost(0, (len(arrays) + len(groups)) * shape[0] * shape[1] * 2),
    )(*arrays)


def body(queries, keys, values, gate_pre, grad_out, w_query, w_key, w_value, w_gate, w_out):
    seq_count, rows, columns = queries.shape
    head_count = columns // HD
    features = grad_out.shape[2]
    peers = lax.axis_size("head")
    factor = (lax.axis_size("seq") * rows) ** (-0.5)
    bf16, f32 = jnp.bfloat16, jnp.float32
    state_shape = (seq_count, head_count, HD, HD)
    cube = (seq_count, rows, columns)

    here = lax.axis_index("head")
    y, lane = here // 2, here % 2
    places = jnp.arange(8, dtype=jnp.int32)
    offset = places % 4
    offset = offset ^ (offset >> 1)
    table = 2 * (y ^ offset) + jnp.where(places < 4, 1 - lane, lane)
    table = table.astype(jnp.int32)

    def along_y(x, by):
        return lax.ppermute(x, "head", [(i, i ^ (2 * by)) for i in range(peers)])

    def other_core(x):
        return lax.ppermute(x, "head", [(i, i ^ 1) for i in range(peers)])

    g0, g1 = grad_out[0], grad_out[1]
    a0 = along_y(g0, 1)
    b1 = along_y(g1, 3)
    a1 = along_y(g1, 1)
    b0 = along_y(g0, 3)
    c0 = along_y(a0, 3)
    c1 = along_y(b1, 1)

    w_pick = pl.pallas_call(
        pick_kernel,
        out_shape=jax.ShapeDtypeStruct((4, columns, features), bf16),
        grid_spec=pltpu.PrefetchScalarGridSpec(
            num_scalar_prefetch=1,
            grid=(4,),
            in_specs=[pl.BlockSpec((columns, features), lambda k, t: (0, t[k]))],
            out_specs=pl.BlockSpec((1, columns, features), lambda k, t: (k, 0, 0)),
        ),
        compiler_params=params(),
        cost_estimate=cost(0, 2 * 4 * columns * features * 2),
    )(table, w_out)
    w_theirs = other_core(w_pick)

    key_state = pl.pallas_call(
        key_state_kernel,
        out_shape=jax.ShapeDtypeStruct(state_shape, bf16),
        compiler_params=params(),
        cost_estimate=cost(2 * seq_count * rows * columns * HD, 4 * seq_count * rows * columns),
    )(keys, values)

    flat = (rows, features)
    two = [jax.ShapeDtypeStruct(cube, f32)] * 2
    piece_flops = 4 * seq_count * rows * features * columns
    mine, other = pl.pallas_call(
        gated_start_kernel,
        out_shape=two,
        grid_spec=pltpu.PrefetchScalarGridSpec(
            num_scalar_prefetch=1,
            grid=(3,),
            in_specs=[whole(grad_out.shape)]
            + [whole(flat)] * 4
            + [
                pl.BlockSpec((columns, features), lambda k, t: (0, t[4 + k])),
                pl.BlockSpec((1, columns, features), lambda k, t: (k, 0, 0)),
            ],
            out_specs=[whole(cube)] * 2,
        ),
        compiler_params=params(),
        cost_estimate=cost(3 * piece_flops, 4 * 1024 * 1024),
    )(table, grad_out, a0, a1, b0, b1, w_out, w_theirs)
    mine, other = pl.pallas_call(
        gated_end_kernel,
        out_shape=two,
        grid_spec=pltpu.PrefetchScalarGridSpec(
            num_scalar_prefetch=1,
            grid=(1,),
            in_specs=[whole(cube)] * 2
            + [whole(flat)] * 2
            + [
                pl.BlockSpec((columns, features), lambda k, t: (0, t[7])),
                pl.BlockSpec((1, columns, features), lambda k, t: (3, 0, 0)),
            ],
            out_specs=[whole(cube)] * 2,
        ),
        compiler_params=params(),
        cost_estimate=cost(piece_flops, 3 * 1024 * 1024),
    )(table, mine, other, c0, c1, w_out, w_theirs)
    theirs = other_core(other)

    d_output, slope, query_state = pl.pallas_call(
        gate_kernel,
        out_shape=[
            jax.ShapeDtypeStruct(cube, bf16),
            jax.ShapeDtypeStruct(cube, f32),
            jax.ShapeDtypeStruct(state_shape, bf16),
        ],
        compiler_params=params(),
        cost_estimate=cost(2 * seq_count * rows * columns * HD, 3 * 1024 * 1024),
    )(mine, theirs, gate_pre, queries)
    prefix = across_seq(key_state, False, query_state)
    suffix = across_seq(query_state, True)

    block = pl.BlockSpec((1, rows, HD), lambda s, h: (s, 0, h))
    d_query, d_gate, dk_part, dv_part = pl.pallas_call(
        make_inner_kernel(factor),
        out_shape=[jax.ShapeDtypeStruct(cube, kind) for kind in (bf16, bf16, f32, f32)],
        grid=(seq_count, head_count),
        in_specs=[block] * 5 + [pl.BlockSpec((1, 1, HD, HD), lambda s, h: (s, h, 0, 0))],
        out_specs=[block] * 4,
        compiler_params=params(),
        cost_estimate=cost(12 * seq_count * rows * rows * columns, 3 * 1024 * 1024),
    )(queries, keys, values, d_output, slope, prefix)

    def project(first):
        weight = pl.BlockSpec((features, columns), lambda k, t: (t[first + k], 0))
        return pl.pallas_call(
            make_project_kernel(factor),
            out_shape=jax.ShapeDtypeStruct((4, seq_count, rows, features), bf16),
            grid_spec=pltpu.PrefetchScalarGridSpec(
                num_scalar_prefetch=1,
                grid=(4,),
                in_specs=[whole(cube)] * 6 + [whole(state_shape)] + [weight] * 4,
                out_specs=pl.BlockSpec((1, seq_count, rows, features), lambda k, t: (k, 0, 0, 0)),
                scratch_shapes=[pltpu.VMEM(cube, bf16)] * 2,
            ),
            compiler_params=params(),
            cost_estimate=cost(32 * seq_count * rows * columns * features, 8 * 1024 * 1024),
        )(table, d_query, d_gate, dk_part, dv_part, keys, values, suffix, w_query, w_key, w_value, w_gate)

    theirs = other_core(project(0))
    own = project(4)

    def chip(place, s):
        return [(own, place, s), (theirs, place, s)]

    far0, far1 = sums([chip(3, 0), chip(3, 1)], flat)
    through0 = along_y(far0, 1)
    through1 = along_y(far1, 3)
    near0, near1 = sums([chip(1, 0), chip(2, 1)], flat)
    direct0 = along_y(near0, 1)
    direct1 = along_y(near1, 3)
    (last0,) = sums([chip(2, 0) + [through0]], flat)
    (last1,) = sums([chip(1, 1) + [through1]], flat)
    joined0 = along_y(last0, 3)
    joined1 = along_y(last1, 1)
    return sums([chip(0, 0) + [direct0, joined0], chip(0, 1) + [direct1, joined1]], flat, stacked=True)


def solution(mesh):
    tokens = P(None, "seq", "head")
    return jax.shard_map(
        body,
        mesh=mesh,
        in_specs=(tokens,) * 5 + (P(None, "head"),) * 4 + (P("head", None),),
        out_specs=tokens,
        check_vma=False,
    )
```
